32 devices in a mesh: box: 2 (over y), gx: 8 (over z, x), gy: 2 (over core).
Axes of the slice: x: 2, y: 2, z: 4, core: 2. Of those that a mesh axis runs over, the one named last changes fastest.
Arguments:
- positions: float32 [16, 4, 3, 256], P(('box', 'gx'), 'gy'), parts along dimension 0, may hold values from 0 to 18, as said below
- polarizability: float32 [16, 4, 256], P(('box', 'gx'), 'gy'), parts along dimension 0, may hold values from 0.3 to 1.5
- tile_counts: int32 [16, 4, 2], P(('box', 'gx'), 'gy'), parts along dimension 0, may hold values from 80 to 128, as said below
- molecules: int32 [16, 4, 256], P(('box', 'gx'), 'gy'), parts along dimension 0, may hold values from 0 to 170, as said below
- perm_field: float32 [16, 4, 3, 256], P(('box', 'gx'), 'gy'), parts along dimension 0, may hold values from -6 to 6
- dipoles: float32 [16, 4, 3, 256], P(('box', 'gx'), 'gy'), parts along dimension 0, may hold values from -4 to 4
- past_out: float32 [16, 4, 7, 3, 256], P(('box', 'gx'), 'gy'), parts along dimension 0, may hold values from -4 to 4
- past_res: float32 [16, 4, 7, 3, 256], P(('box', 'gx'), 'gy'), parts along dimension 0, may hold values from -15 to 15
Outputs:
- dipoles_next: float32 [16, 4, 3, 256], P(('box', 'gx'), 'gy'), parts along dimension 0
- diis_weights: float32 [16], P('box'), parts along dimension 0
The draws below stay inside these ranges and needn't reach their ends.
There are 2 independent parts, one for each index of `box`. The reference program is written for one: setup_inputs(seed, part) draws one part's arguments, and reference() takes and returns one part's arrays. A program takes and returns all parts, laid end to end along the dimension named above; each array names one. Nothing has to cross between parts.
Inputs may be any that keep to these rules, and one draw needn't show every extreme that they name: x and y in [0, 9); z of an atom in z-tile t lies in [9 t, 9 t + 9); padded slots carry positions too. `tile_counts`: some z-tile is full. `molecules`: a group holds at most three atoms, all of one z-tile of one cell.
All inputs are finite; a program needn't handle non-finite values.
Results may differ from the reference program's by a relative error of at most 0.0003.
Values sent between devices are 32-bit elements; how exact they have to be, the bound alone decides.
A program may use at most 64 MiB of HBM per device.

```python
import math
import jax
import jax.numpy as jnp
from jax import lax

TILE = 128
TILES = 2
HIST = 8
ITERS = 2
ATOMS = 256
CX = 8
CY = 4


def draw_positions(key, part):
    key_plane, key_height = jax.random.split(jax.random.fold_in(key, 11))
    plane_xy = jax.random.uniform(key_plane, (CX, CY, 2, ATOMS), jnp.float32, 0.0, 9.0)
    height = jax.random.uniform(key_height, (CX, CY, 1, ATOMS), jnp.float32, 0.0, 9.0)
    floor_z = (lax.broadcasted_iota(jnp.int32, (CX, CY, 1, ATOMS), 3) // TILE).astype(jnp.float32) * 9.0
    return jnp.concatenate([plane_xy, height + floor_z], axis=2)


def draw_tile_counts(key, part):
    key_fill, key_full = jax.random.split(jax.random.fold_in(key, 23))
    counts = jax.random.randint(key_fill, (CX * CY * TILES,), TILE - 3 * TILE // 8, TILE + 1)
    full_at = jax.random.randint(key_full, (), 0, CX * CY * TILES)
    return counts.at[full_at].set(TILE).reshape(CX, CY, TILES).astype(jnp.int32)


def draw_molecules(key, part):
    dims_all = (CX, CY, TILES, TILE)
    scores = jax.random.randint(jax.random.fold_in(key, 37), dims_all, 0, 1 << 20)
    scores = scores * TILE + lax.broadcasted_iota(jnp.int32, dims_all, 3)
    shuffled = jnp.argsort(scores, axis=3, stable=True).astype(jnp.int32)
    tile_base = lax.broadcasted_iota(jnp.int32, dims_all, 2) * TILE
    return (tile_base + shuffled // 3).reshape(CX, CY, ATOMS)


def draw_past_res(key, part):
    key_private = jax.random.fold_in(jax.random.fold_in(key, 41), 0)
    dims_all = (CX, CY, HIST - 1, 3, ATOMS)
    along_x = lax.broadcasted_iota(jnp.float32, dims_all, 0) / max(CX - 1, 1)
    values = 3.0 ** along_x * jnp.clip(jax.random.normal(key_private, dims_all, jnp.float32), -4.0, 4.0)
    return jnp.clip(values, -15.0, 15.0)


def block_levels(stream_key, shape, cuts, least, high):
    level = 1.0
    for dim, parts in cuts:
        steps = jax.random.uniform(jax.random.fold_in(jax.random.fold_in(stream_key, 6), dim), (parts,), jnp.float32, least / len(cuts), high / len(cuts))
        level = level * jnp.repeat(jnp.exp(steps), shape[dim] // parts).reshape((-1,) + (1,) * (len(shape) - 1 - dim))
    return level


def gaussian(own_key, dims, spread, most, cuts=(), held_as=jnp.bfloat16):
    values = spread * jax.random.normal(own_key, dims, jnp.float32)
    if cuts:
        values = values * block_levels(own_key, dims, cuts, -0.22, 0.18)
    return jnp.clip(values, -most, most).astype(held_as)


def setup_inputs(seed: int = 0, part: int = 0) -> dict:
    seeds = jax.random.split(jax.random.key(seed), 9)
    part_splits = jax.random.split(jax.random.fold_in(seeds[8], part), 9)
    return {
        "positions": draw_positions(jax.random.fold_in(jax.random.fold_in(seeds[8], part), 71), part),
        "polarizability": jnp.clip(jnp.exp(math.log(1.5) - 1.60943787 * jax.random.uniform(part_splits[1], (CX, CY, ATOMS), jnp.float32) ** block_levels(part_splits[1], (CX, CY, ATOMS), ((0, 8), (1, 2)), -0.2, 0.2)), 0.3, 1.5),
        "tile_counts": draw_tile_counts(jax.random.fold_in(jax.random.fold_in(seeds[8], part), 71), part),
        "molecules": draw_molecules(jax.random.fold_in(jax.random.fold_in(seeds[8], part), 71), part),
        "perm_field": gaussian(part_splits[4], (CX, CY, 3, ATOMS), 1.0, 6.0, ((0, 8), (1, 2)), jnp.float32),
        "dipoles": gaussian(part_splits[5], (CX, CY, 3, ATOMS), 0.5, 4.0, ((0, 8), (1, 2)), jnp.float32),
        "past_out": gaussian(part_splits[6], (CX, CY, HIST - 1, 3, ATOMS), 0.5, 4.0, ((0, 8), (1, 2)), jnp.float32),
        "past_res": draw_past_res(jax.random.fold_in(jax.random.fold_in(seeds[8], part), 71), part),
    }


CELL_SIDE = 9.0
CUTOFF_SQ = 81.0
SOFTENING = 0.25
THOLE_DAMP = 0.39
FAR_LIFT = 1000.0

def pair_terms(target_coords, target_polar, target_groups, target_occupied, source_coords, source_polar, source_groups, source_occupied):
    displace = source_coords[:, None, :] - target_coords[:, :, None]
    square_dist = lax.optimization_barrier(jnp.sum(displace * displace, axis=0)) + SOFTENING
    distance = jnp.sqrt(square_dist)
    cube_dist = square_dist * distance
    damped = THOLE_DAMP * cube_dist / jnp.sqrt(target_polar[:, None] * source_polar[None, :])
    damping = jnp.exp(-damped)
    tapering = jnp.square(jnp.maximum(1.0 - square_dist / CUTOFF_SQ, 0.0))
    keeper = (target_groups[:, None] != source_groups[None, :]).astype(jnp.float32)
    weight = tapering * keeper * target_occupied[:, None] * source_occupied[None, :]
    isotropic = weight * -jnp.expm1(-damped) / cube_dist
    tensorial = 3.0 * weight * (1.0 - (1.0 + damped) * damping) / (cube_dist * square_dist)
    return (displace, isotropic, tensorial)

def field_targets(displace, isotropic, tensorial, source_dipole):
    projected = lax.optimization_barrier(jnp.sum(displace * source_dipole[:, None, :], axis=0))
    return lax.optimization_barrier(jnp.sum(displace * (tensorial * projected)[None], axis=2)) - lax.optimization_barrier(jnp.sum(isotropic[None] * source_dipole[:, None, :], axis=2))

def tiled(values, filler, tile_count):
    shaped = values.reshape(values.shape[:-1] + (tile_count, values.shape[-1] // tile_count))
    widths = [(0, 0)] * (shaped.ndim - 2) + [(1, 1), (0, 0)]
    return jnp.pad(shaped, widths, constant_values=filler)

def padded_coords(coords, tile_count):
    marker = tiled(jnp.zeros_like(coords), 1.0, tile_count)
    lifted = jnp.array([0.0, 0.0, FAR_LIFT], jnp.float32).reshape(3, 1, 1)
    return tiled(coords, 0.0, tile_count) + marker * lifted

def band_sources(padded, tile_at):
    coords, polarity, groups, occupied, dipole = padded

    def flat_vector(member):
        window_part = lax.dynamic_slice_in_dim(member, tile_at, 3, 2)
        return jnp.transpose(window_part, (1, 0, 2, 3)).reshape(3, -1)

    def flat_scalar(member):
        return lax.dynamic_slice_in_dim(member, tile_at, 3, 1).reshape(-1)
    return (flat_vector(coords), flat_scalar(polarity), flat_scalar(groups), flat_scalar(occupied), flat_vector(dipole))

def band_field(own_cell, padded, tile_count):
    coords, polarity, groups, occupied = own_cell
    tile_width = coords.shape[-1] // tile_count

    def one_tile(tile_at):
        first_slot = tile_at * tile_width
        source_coords, source_polar, source_groups, source_occupied, source_dipole = band_sources(padded, tile_at)
        displace, isotropic, tensorial = pair_terms(lax.dynamic_slice_in_dim(coords, first_slot, tile_width, 1), lax.dynamic_slice_in_dim(polarity, first_slot, tile_width, 0), lax.dynamic_slice_in_dim(groups, first_slot, tile_width, 0), lax.dynamic_slice_in_dim(occupied, first_slot, tile_width, 0), source_coords, source_polar, source_groups, source_occupied)
        return field_targets(displace, isotropic, tensorial, source_dipole)
    fields = lax.map(one_tile, jnp.arange(tile_count, dtype=jnp.int32))
    return jnp.transpose(fields, (1, 0, 2)).reshape(3, -1)

def field_on(positions, polarizability, molecules, occupied, dipole):
    gathered = ([], [], [], [], [])
    for shift_x in (-1, 0, 1):
        for shift_y in (-1, 0, 1):

            def rolled(values):
                return jnp.roll(values, (-shift_x, -shift_y), axis=(0, 1))
            lifted = jnp.array([CELL_SIDE * shift_x, CELL_SIDE * shift_y, 0.0], jnp.float32).reshape(3, 1)
            gathered[0].append(rolled(positions) + lifted)
            gathered[1].append(rolled(polarizability))
            if shift_x == 0 and shift_y == 0:
                gathered[2].append(molecules)
            else:
                gathered[2].append(jnp.full_like(molecules, -1))
            gathered[3].append(rolled(occupied))
            gathered[4].append(rolled(dipole))
    padded = (padded_coords(jnp.stack(gathered[0], 2), TILES), tiled(jnp.stack(gathered[1], 2), 1.0, TILES), tiled(jnp.stack(gathered[2], 2), -1, TILES), tiled(jnp.stack(gathered[3], 2), 0.0, TILES), tiled(jnp.stack(gathered[4], 2), 0.0, TILES))
    cell_total = CX * CY
    flat_padded = tuple((member.reshape((cell_total,) + member.shape[2:]) for member in padded))
    flat_own = tuple((member.reshape((cell_total,) + member.shape[2:]) for member in (positions, polarizability, molecules, occupied)))

    def per_cell(both_parts):
        return band_field(both_parts[0], both_parts[1], TILES)
    fields = lax.map(per_cell, (flat_own, flat_padded))
    return fields.reshape(CX, CY, 3, -1)

def diis_weights(gram_matrix):
    lower = jnp.linalg.cholesky(gram_matrix)
    history = gram_matrix.shape[0]
    forward = []
    for row_at in range(history):
        running = jnp.ones((), gram_matrix.dtype)
        for col_at in range(row_at):
            running = running - lower[row_at, col_at] * forward[col_at]
        forward.append(running / lower[row_at, row_at])
    backward = [None] * history
    for row_at in reversed(range(history)):
        running = forward[row_at]
        for col_at in range(row_at + 1, history):
            running = running - lower[col_at, row_at] * backward[col_at]
        backward[row_at] = running / lower[row_at, row_at]
    solved = jnp.stack(backward)
    return solved / jnp.sum(solved)

def reference(positions, polarizability, tile_counts, molecules, perm_field, dipoles, past_out, past_res):
    slot_index = lax.broadcasted_iota(jnp.int32, (CX, CY, TILES, TILE), 3)
    occupied = (slot_index < tile_counts[:, :, :, None]).astype(jnp.float32).reshape(CX, CY, ATOMS)
    occupied_vec = occupied[:, :, None, :]
    current = dipoles * occupied_vec
    stored_out = jnp.moveaxis(past_out, 2, 0) * occupied_vec
    stored_res = jnp.moveaxis(past_res, 2, 0) * occupied_vec
    scaled = (polarizability * occupied)[:, :, None, :]
    weights = jnp.zeros((HIST,), jnp.float32)
    for step_at in range(ITERS):
        induced = field_on(positions, polarizability, molecules, occupied, current)
        jacobi = scaled * (perm_field + induced)
        residual = jacobi - current
        outputs_all = jnp.concatenate([stored_out, jacobi[None]], 0)
        residual_all = jnp.concatenate([stored_res, residual[None]], 0)
        flattened = residual_all.reshape(HIST, -1)
        gram_matrix = jnp.dot(flattened.astype(jnp.float32), flattened.T.astype(jnp.float32), precision=lax.Precision.HIGHEST, preferred_element_type=jnp.float32)
        weights = diis_weights(gram_matrix)
        current = lax.optimization_barrier(jnp.sum(weights[:, None, None, None, None] * outputs_all, axis=0))
        stored_out = outputs_all[1:]
        stored_res = residual_all[1:]
    return (current, weights)
```

```python
import functools

import jax
import jax.numpy as jnp
from jax import lax
from jax.experimental import pallas as pl
from jax.experimental.pallas import tpu as pltpu
from jax.sharding import PartitionSpec as P

CELL_SIDE = 9.0
CUTOFF_SQ = 81.0
SOFTENING = 0.25
THOLE_DAMP = 0.39
LANES = 128
SUBLANES = 8
ROWS = 32
DEPTH = 48
SPLITS = 3
TERMS = 16
MESH = pl.DeviceIdType.MESH

BLOCKS = ((0, 0), (0, 1), (1, 0), (1, 1), (-1, 0), (-1, 1))


def block_row(cell, half, cells):
    if half == 0:
        return cell
    return -1 if cell == cells - 1 else cells


def kernel(
    nx,
    ny,
    cells,
    slots,
    tile_width,
    args,
    outs,
    held,
    stat,
    out_hist,
    res_hist,
    scale,
    stat_halo,
    hist_halo,
    jac_halo,
    place,
    near,
    spread,
    group,
    pull,
    pair,
    jac_own,
    vec,
    past_send,
    past_recv,
    row_send,
    row_recv,
    in_sem,
    stat_sem,
    hist_sem,
    jac_sem,
    past_sem,
    row_sem,
):
    next_ref, weight_ref = outs
    positions, polarity, molecules, permanent, dipoles, past_out, past_res, counts = held
    tiles = slots // LANES
    width = cells * 3 * slots
    total = nx * ny
    my_x = lax.axis_index("gx")
    my_y = lax.axis_index("gy")
    me = my_x * ny + my_y

    def other(step):
        flat = lax.rem(me + step, total)
        return {"gx": flat // ny, "gy": lax.rem(flat, ny)}

    barrier = pltpu.get_barrier_semaphore()

    fetches = [
        pltpu.make_async_copy(arg.at[0], into, in_sem.at[at])
        for at, (arg, into) in enumerate(zip(args, held))
    ]
    for fetch in fetches:
        fetch.start()

    def greet(step, carry):
        pl.semaphore_signal(barrier, inc=1, device_id=other(step), device_id_type=MESH)
        return carry

    lax.fori_loop(1, total, greet, 0)

    def halo_copies(source, landing, sems):
        copies = []
        for at, (x_offset, half) in enumerate(BLOCKS[1:]):
            target = {
                "gx": lax.rem(my_x - x_offset + nx, nx),
                "gy": lax.rem(my_y + half, ny),
            }
            copies.append(
                pltpu.make_async_remote_copy(
                    src_ref=source,
                    dst_ref=landing.at[at],
                    send_sem=sems.at[0, at],
                    recv_sem=sems.at[1, at],
                    device_id=target,
                    device_id_type=MESH,
                )
            )
        return copies

    index = lax.broadcasted_iota(jnp.int32, (1, slots), 1)
    for fetch in fetches:
        fetch.wait()
    occupied = []
    for cell in range(cells):
        live = jnp.zeros((1, slots), jnp.float32)
        for tile in range(slots // tile_width):
            first = tile * tile_width
            inside = jnp.logical_and(index >= first, index < first + counts[cell, tile])
            live = jnp.where(inside, 1.0, live)
        occupied.append(live)

    for cell in range(cells):
        span = slice(cell * slots, (cell + 1) * slots)
        polar = polarity[cell : cell + 1, :]
        for m in range(3):
            stat[m : m + 1, span] = positions[m, cell : cell + 1, :]
            stat[4 + m : 5 + m, span] = dipoles[m, cell : cell + 1, :] * occupied[cell]
        stat[3:4, span] = lax.rsqrt(polar)
        stat[7:8, span] = molecules[cell : cell + 1, :].astype(jnp.float32)
        scale[0:1, span] = polar * occupied[cell]

    for stored, hist in ((past_res, res_hist), (past_out, out_hist)):
        hist[SUBLANES - 1 :, :] = jnp.zeros((1, width), jnp.float32)
        for cell in range(cells):
            for m in range(3):
                first = (cell * 3 + m) * slots
                for k in range(SUBLANES - 1):
                    row = stored[k, m, cell : cell + 1, :] * occupied[cell]
                    hist[k : k + 1, first : first + slots] = row

    wide = lax.broadcasted_iota(jnp.int32, (SUBLANES, slots), 0)
    centre = CELL_SIDE * 0.5

    def split(values):
        high = values.astype(jnp.bfloat16)
        rest = values - high.astype(jnp.float32)
        mid = rest.astype(jnp.bfloat16)
        low = (rest - mid.astype(jnp.float32)).astype(jnp.bfloat16)
        return high, mid, low

    def located(rows, x_shift, y_shift):
        shift = jnp.where(wide == 0, x_shift - centre, jnp.where(wide == 1, y_shift - cells * centre, -tiles * centre))
        moved = jnp.where(wide < 3, rows + shift, 0.0)
        return moved, jnp.sum(moved * moved, axis=0, keepdims=True)

    def in_row(at, value, rows):
        return jnp.where(wide == at, value, rows)

    def prepare(block, block_stat):
        x_offset, half = BLOCKS[block]
        for cell in range(cells):
            rows = block_stat[:, cell * slots : (cell + 1) * slots]
            moved, norm = located(rows, CELL_SIDE * x_offset, CELL_SIDE * block_row(cell, half, cells))
            place[block, cell] = moved
            high, mid, low = (part.astype(jnp.float32) for part in split(in_row(3, norm, moved)))
            high_one, mid_one = in_row(3, 1.0, high), in_row(3, 1.0, mid)
            stack = jnp.concatenate([high, mid, high_one, low, high_one, mid_one, rows], axis=0)
            columns = jnp.transpose(stack)
            near[block, cell] = columns[:, :DEPTH].astype(jnp.bfloat16)
            spread[block, cell] = jnp.broadcast_to(columns[:, DEPTH + 3 : DEPTH + 4], (slots, LANES))
            if block == 0:
                group[cell] = jnp.broadcast_to(columns[:, DEPTH + 7 : DEPTH + 8], (slots, LANES))

    def lines(block, cell, vector):
        bx, by, bz = (place[block, cell, m : m + 1, :] for m in range(3))
        vx, vy, vz = (3.0 * v for v in vector)
        dot = bx * vx + by * vy + bz * vz
        kind = jnp.bitwise_and(wide, 3)
        right = jnp.where(kind == 0, dot, jnp.where(kind == 1, vx, jnp.where(kind == 2, vy, vz)))
        upper = wide < 4
        outer = jnp.concatenate(
            [jnp.where(upper, 1.0, bx) * right, jnp.where(upper, by, bz) * right], axis=0
        )
        ux, uy, uz = vector
        plain = jnp.concatenate(
            [in_row(4, -ux, 0.0), in_row(0, -uy, in_row(4, -uz, 0.0))], axis=0
        )
        for at, part in enumerate(zip(split(outer), split(plain))):
            for which, term in enumerate(part):
                for copy in range(2):
                    first = (2 * which + copy) * slots
                    pull[block, cell, at * TERMS : (at + 1) * TERMS, first : first + slots] = term

    def toward(target):
        rows = stat[:, target * slots : (target + 1) * slots]
        moved, norm = located(rows, 0.0, CELL_SIDE * target)
        high, mid, low = (part.astype(jnp.float32) for part in split(in_row(3, 0.0, -2.0 * moved)))
        norm_parts = [part.astype(jnp.float32) for part in split(norm + SOFTENING)]
        high_one = in_row(3, 1.0, high)
        stack = jnp.concatenate(
            [
                high_one,
                high_one,
                in_row(3, norm_parts[1], mid),
                high_one,
                in_row(3, norm_parts[2], low),
                in_row(3, norm_parts[0], mid),
            ],
            axis=0,
        )
        return stack.astype(jnp.bfloat16)

    prepare(0, stat)
    reach = [toward(c) for c in range(cells)]
    damp = [-THOLE_DAMP * stat[3:4, c * slots : (c + 1) * slots] for c in range(cells)]

    sub = lax.broadcasted_iota(jnp.int32, (SUBLANES, LANES), 0)
    lane = lax.broadcasted_iota(jnp.int32, (SUBLANES, LANES), 1)
    chunks = [slice(at * LANES, (at + 1) * LANES) for at in range(width // LANES)]

    def inner(rows, vector):
        parts = [r * v for r, v in zip(rows, vector)]
        while len(parts) > 1:
            parts = [sum(parts[at : at + 2]) for at in range(0, len(parts), 2)]
        return jnp.sum(parts[0], axis=1, keepdims=True)

    hist_rows = [res_hist[:, chunk] for chunk in chunks]
    past_gram = jnp.zeros((SUBLANES, LANES), jnp.float32)
    for k in range(SUBLANES - 1):
        column = inner(hist_rows, [rows[k : k + 1] for rows in hist_rows])
        past_gram = past_gram + jnp.where(lane == k, column, 0.0)

    met = [
        (block, cell, c, block == 0 and cell == c)
        for block in range(len(BLOCKS))
        for c in range(cells)
        for cell in range(cells)
        if (BLOCKS[block][1] == 0 or cell in (0, cells - 1))
        and abs(block_row(cell, BLOCKS[block][1], cells) - c) <= 1
    ]

    def share(mine, sent, landed, sems):
        sent[...] = mine

        def copy_to(step):
            return pltpu.make_async_remote_copy(
                src_ref=sent,
                dst_ref=landed.at[step - 1],
                send_sem=sems.at[0],
                recv_sem=sems.at[1],
                device_id=other(step),
                device_id_type=MESH,
            )

        def send(step, carry):
            copy_to(step).start()
            return carry

        def start():
            lax.fori_loop(1, total, send, 0)

        def finish():
            pltpu.make_async_copy(landed, landed, sems.at[1]).wait()
            return mine + jnp.sum(landed[...], axis=0)

        def sent_all():
            pltpu.make_async_copy(landed, landed, sems.at[0]).wait()

        return start, finish, sent_all

    start_past, finish_past, past_sent = share(past_gram, past_send, past_recv, past_sem)
    hist_copies = halo_copies(out_hist, hist_halo, hist_sem)

    def pair_terms(at):
        block, cell, c, same = met[at]

        def some(step, carry):
            first = pl.multiple_of(step * ROWS, ROWS)
            local = pl.ds(first, ROWS)
            s = jnp.dot(near[block, cell, local, :], reach[c], preferred_element_type=jnp.float32)
            bn = spread[block, cell, local, :]
            bn = jnp.concatenate([bn] * tiles, axis=1)
            inv = lax.rsqrt(s)
            inv2 = inv * inv
            minus_x = (s * s) * inv * (damp[c] * bn)
            e = jnp.exp(minus_x)
            t = jnp.maximum(CUTOFF_SQ - s, 0.0)
            w = t * t * (inv2 * inv)
            if same:
                mine = stat[7:8, c * slots : (c + 1) * slots]
                theirs = jnp.concatenate([group[cell, local, :]] * tiles, axis=1)
                w = jnp.where(mine != theirs, w, 0.0)
            rest = 1.0 - e
            for which, term in enumerate((w * inv2 * (rest + minus_x * e), w * rest)):
                high = term.astype(jnp.bfloat16)
                low = (term - high.astype(jnp.float32)).astype(jnp.bfloat16)
                pair[at, pl.ds(pl.multiple_of(2 * which * slots + first, ROWS), ROWS), :] = high
                pair[at, pl.ds(pl.multiple_of((2 * which + 1) * slots + first, ROWS), ROWS), :] = low
            return carry

        lax.fori_loop(0, slots // ROWS, some, 0, unroll=True)

    def pulled(at, sums):
        block, cell, c, _ = met[at]
        part = jnp.dot(pull[block, cell], pair[at], preferred_element_type=jnp.float32)
        sums[c] = part if sums[c] is None else sums[c] + part

    def jacobi_rows(sums):
        found = []
        kind = jnp.bitwise_and(wide, 3)
        for c in range(cells):
            span = slice(c * slots, (c + 1) * slots)
            ax, ay, az = (place[0, c, m : m + 1, :] for m in range(3))
            total_sum = sum(sums[c][at * TERMS : (at + 1) * TERMS] for at in range(SPLITS))
            turn = jnp.where(kind == 0, 1.0, jnp.where(kind == 1, -ax, jnp.where(kind == 2, -ay, -az)))
            folded = [total_sum[at : at + SUBLANES] * turn for at in (0, SUBLANES)]
            base, hx, hy, hz = (
                jnp.sum(jnp.where((wide < 4) == side, part, 0.0), axis=0, keepdims=True)
                for part in folded
                for side in (True, False)
            )
            for m, (h, a) in enumerate(((hx, ax), (hy, ay), (hz, az))):
                field = permanent[m, c : c + 1, :] + (h - a * base) * (1.0 / CUTOFF_SQ**2)
                row = scale[0:1, span] * field
                for tile in range(tiles):
                    found.append(row[:, tile * LANES : (tile + 1) * LANES])
        return found

    def as_row(column):
        return jnp.sum(jnp.where(sub == lane, column, 0.0), axis=0, keepdims=True)

    def mirrored(gram, row, k):
        column = jnp.sum(jnp.where(sub == lane, row, 0.0), axis=1, keepdims=True)
        return jnp.where(lane == k, column, jnp.where(sub == k, row, gram))

    def solve(gram):
        held = jnp.where(lane == SUBLANES, 1.0, gram)
        for k in range(SUBLANES):
            column = jnp.broadcast_to(held[:, k : k + 1], held.shape)
            pivot_row = held[k : k + 1, :] / column[k : k + 1, :]
            held = jnp.where(sub == k, pivot_row, held - column * pivot_row)
        y = jnp.broadcast_to(held[:, SUBLANES : SUBLANES + 1], held.shape)
        return y / jnp.sum(y, axis=0, keepdims=True)

    def mixed(hist, weights, chunk):
        return jnp.sum(weights * hist, axis=0, keepdims=True)

    newest = SUBLANES - 1
    pl.semaphore_wait(barrier, total - 1)
    stat_copies = halo_copies(stat, stat_halo, stat_sem)
    for copy in stat_copies:
        copy.start()

    sums = [None] * cells
    waiting = []
    for block in range(len(BLOCKS)):
        if block:
            stat_copies[block - 1].wait_recv()
            prepare(block, stat_halo.at[block - 1])
        if block == len(BLOCKS) - 2:
            start_past()
            for copy in hist_copies:
                copy.start()
        block_stat = stat_halo.at[block - 1] if block else stat
        for cell in range(cells):
            lines(block, cell, [block_stat[4 + m : 5 + m, cell * slots : (cell + 1) * slots] for m in range(3)])
        for at in range(len(met)):
            if met[at][0] == block:
                pair_terms(at)
                waiting.append(at)
                if len(waiting) > 1:
                    pulled(waiting.pop(0), sums)
    for at in waiting:
        pulled(at, sums)

    jacobi = jacobi_rows(sums)
    for row, chunk in zip(jacobi, chunks):
        jac_own[0:1, chunk] = row
    jac_copies = halo_copies(jac_own, jac_halo, jac_sem)
    residual = []
    for at, chunk in enumerate(chunks):
        cell, rest = divmod(at, 3 * tiles)
        m, tile = divmod(rest, tiles)
        first = cell * slots + tile * LANES
        residual.append(jacobi[at] - stat[4 + m : 5 + m, first : first + LANES])
    res_rows = [jnp.where(sub == newest, r, rows) for r, rows in zip(residual, hist_rows)]
    row = as_row(inner(res_rows, residual))
    start, finish, first_sent = share(row, row_send.at[0], row_recv.at[0], row_sem.at[0])
    for copy in jac_copies:
        copy.start()
    start()
    past_gram = finish_past()
    gram = mirrored(past_gram, finish(), newest)
    weights = solve(gram)

    current = []
    for at, chunk in enumerate(chunks):
        row = mixed(out_hist[:, chunk], weights, chunk) + weights[newest : newest + 1] * jacobi[at]
        current.append(row)
        vec[0:1, chunk] = row
    for block in range(1, len(BLOCKS)):
        hist_copies[block - 1].wait_recv()
        jac_copies[block - 1].wait_recv()
        for chunk in chunks:
            vec[block : block + 1, chunk] = (
                mixed(hist_halo[block - 1, :, chunk], weights, chunk)
                + weights[newest : newest + 1] * jac_halo[block - 1, 0:1, chunk]
            )
    for block in range(len(BLOCKS)):
        for cell in range(cells):
            starts = [(cell * 3 + m) * slots for m in range(3)]
            lines(block, cell, [vec[block : block + 1, at : at + slots] for at in starts])
    sums = [None] * cells
    for at in range(len(met)):
        pulled(at, sums)

    jacobi_next = jacobi_rows(sums)
    residual = [a - b for a, b in zip(jacobi_next, current)]
    res_rows = [jnp.where(sub == 0, r, rows) for r, rows in zip(residual, res_rows)]
    row = as_row(inner(res_rows, residual))
    start, finish, second_sent = share(row, row_send.at[1], row_recv.at[1], row_sem.at[1])
    start()
    gram = mirrored(gram, finish(), 0)
    weights = solve(gram)
    kept = jnp.where(sub == 0, 0.0, weights)
    for at, chunk in enumerate(chunks):
        cell, rest = divmod(at, 3 * tiles)
        m, tile = divmod(rest, tiles)
        next_ref[0, m, cell : cell + 1, tile * LANES : (tile + 1) * LANES] = (
            mixed(out_hist[:, chunk], kept, chunk)
            + weights[newest : newest + 1] * jac_own[0:1, chunk]
            + weights[0:1] * jacobi_next[at]
        )
    column = jnp.concatenate([weights[1:], weights[0:1]], axis=0)
    weight_ref[...] = as_row(column)[0, :SUBLANES]

    for copy in stat_copies + hist_copies + jac_copies:
        copy.wait_send()
    past_sent()
    first_sent()
    second_sent()


def wired(arg_count, nx, ny, cells, slots, tile_width, counts_arg, *refs):
    args, rest = refs[:arg_count], refs[arg_count:]
    outs, rest = rest[:2], rest[2:]
    held, rest = rest[:arg_count], rest[arg_count:]
    counts, *rest = rest
    args, inside = (*args, counts_arg), (*held, counts)
    kernel(nx, ny, cells, slots, tile_width, args, outs, inside, *rest)


def body(nx, ny, positions, polarizability, tile_counts, molecules, perm_field, dipoles, past_out, past_res):
    cells, tile_count = tile_counts.shape[1:]
    slots = positions.shape[-1]
    tile_width = slots // tile_count
    tiles = slots // LANES
    past = past_out.shape[2]
    assert ny == 2 and nx > 2 and cells > 1 and past + 1 == SUBLANES and slots % LANES == 0
    width = cells * 3 * slots

    halo = len(BLOCKS) - 1
    met = 3 * (3 * cells)
    vmem = pl.BlockSpec(memory_space=pltpu.VMEM)
    hbm = pl.BlockSpec(memory_space=pltpu.HBM)
    raw = (
        jnp.swapaxes(positions, 1, 2),
        polarizability,
        molecules,
        jnp.swapaxes(perm_field, 1, 2),
        jnp.swapaxes(dipoles, 1, 2),
        jnp.transpose(past_out, (0, 2, 3, 1, 4)),
        jnp.transpose(past_res, (0, 2, 3, 1, 4)),
    )
    tile_counts, *raw = (
        pltpu.with_memory_space_constraint(arg, pltpu.HBM) for arg in (tile_counts, *raw)
    )
    pairs_kept = met * slots * slots
    current, weights = pl.pallas_call(
        functools.partial(wired, len(raw), nx, ny, cells, slots, tile_width),
        out_shape=(
            jax.ShapeDtypeStruct((1, 3, cells, slots), jnp.float32),
            jax.ShapeDtypeStruct((SUBLANES,), jnp.float32),
        ),
        in_specs=[hbm] * (1 + len(raw)),
        out_specs=(vmem, vmem),
        scratch_shapes=[pltpu.VMEM(arg.shape[1:], arg.dtype) for arg in raw]
        + [
            pltpu.SMEM(tile_counts.shape[1:], tile_counts.dtype),
            pltpu.VMEM((SUBLANES, cells * slots), jnp.float32),
            pltpu.VMEM((SUBLANES, width), jnp.float32),
            pltpu.VMEM((SUBLANES, width), jnp.float32),
            pltpu.VMEM((1, cells * slots), jnp.float32),
            pltpu.VMEM((halo, SUBLANES, cells * slots), jnp.float32),
            pltpu.VMEM((halo, SUBLANES, width), jnp.float32),
            pltpu.VMEM((halo, 1, width), jnp.float32),
            pltpu.VMEM((halo + 1, cells, SUBLANES, slots), jnp.float32),
            pltpu.VMEM((halo + 1, cells, slots, DEPTH), jnp.bfloat16),
            pltpu.VMEM((halo + 1, cells, slots, LANES), jnp.float32),
            pltpu.VMEM((cells, slots, LANES), jnp.float32),
            pltpu.VMEM((halo + 1, cells, SPLITS * TERMS, 4 * slots), jnp.bfloat16),
            pltpu.VMEM((met, 4 * slots, slots), jnp.bfloat16),
            pltpu.VMEM((1, width), jnp.float32),
            pltpu.VMEM((SUBLANES, width), jnp.float32),
            pltpu.VMEM((SUBLANES, LANES), jnp.float32),
            pltpu.VMEM((nx * ny - 1, SUBLANES, LANES), jnp.float32),
            pltpu.VMEM((2, 1, LANES), jnp.float32),
            pltpu.VMEM((2, nx * ny - 1, 1, LANES), jnp.float32),
            pltpu.SemaphoreType.DMA((len(raw) + 1,)),
            pltpu.SemaphoreType.DMA((2, halo)),
            pltpu.SemaphoreType.DMA((2, halo)),
            pltpu.SemaphoreType.DMA((2, halo)),
            pltpu.SemaphoreType.DMA((2,)),
            pltpu.SemaphoreType.DMA((2, 2)),
        ],
        compiler_params=pltpu.CompilerParams(
            collective_id=0, has_side_effects=True, vmem_limit_bytes=32 * 1024 * 1024
        ),
        cost_estimate=pl.CostEstimate(
            flops=70 * pairs_kept, bytes_accessed=16 * width * SUBLANES, transcendentals=2 * pairs_kept
        ),
    )(tile_counts, *raw)
    return (jnp.swapaxes(current, 1, 2), weights)


def solution(mesh):
    cell_axes = P(("box", "gx"), "gy")
    return jax.shard_map(
        functools.partial(body, mesh.shape["gx"], mesh.shape["gy"]),
        mesh=mesh,
        in_specs=(cell_axes,) * 8,
        out_specs=(cell_axes, P("box")),
        check_vma=False,
    )
```

```python
import functools

import jax
import jax.numpy as jnp
from jax import lax
from jax.experimental import pallas as pl
from jax.experimental.pallas import tpu as pltpu
from jax.sharding import PartitionSpec as P

CELL_SIDE = 9.0
CUTOFF_SQ = 81.0
SOFTENING = 0.25
THOLE_DAMP = 0.39
LANES = 128
SUBLANES = 8
ROWS = 32
DEPTH = 48
SPLITS = 3
TERMS = 16
MESH = pl.DeviceIdType.MESH

STAGES = ((0,), (1,), (2, 3), (4, 5))
BLOCKS = ((0, 0), (0, 1), (1, 0), (1, 1), (-1, 0), (-1, 1))


def block_row(cell, half, cells):
    if half == 0:
        return cell
    return -1 if cell == cells - 1 else cells


def kernel(
    nx,
    ny,
    cells,
    slots,
    tile_width,
    args,
    outs,
    held,
    stat,
    out_hist,
    res_hist,
    scale,
    stat_halo,
    hist_halo,
    jac_halo,
    place,
    near,
    spread,
    group,
    pull,
    pair,
    jac_own,
    vec,
    past_send,
    past_recv,
    row_send,
    row_recv,
    in_sem,
    stat_sem,
    hist_sem,
    jac_sem,
    past_sem,
    row_sem,
):
    next_ref, weight_ref = outs
    positions, polarity, molecules, permanent, dipoles, past_out, past_res, counts = held
    tiles = slots // LANES
    width = cells * 3 * slots
    total = nx * ny
    my_x = lax.axis_index("gx")
    my_y = lax.axis_index("gy")
    me = my_x * ny + my_y

    def other(step):
        flat = lax.rem(me + step, total)
        return {"gx": flat // ny, "gy": lax.rem(flat, ny)}

    barrier = pltpu.get_barrier_semaphore()

    few = total <= 2 * SUBLANES

    def to_all(act):
        def both(step, carry):
            act(step)
            act(total - step)
            return carry

        lax.fori_loop(1, total // 2, both, 0, unroll=few)
        act(total // 2)

    to_all(lambda step: pl.semaphore_signal(barrier, inc=1, device_id=other(step), device_id_type=MESH))
    fetches = [
        pltpu.make_async_copy(arg.at[0], into, in_sem.at[at])
        for at, (arg, into) in enumerate(zip(args, held))
    ]
    for fetch in fetches:
        fetch.start()


    def halo_copies(source, landing, sems):
        copies = []
        for at, (x_offset, half) in enumerate(BLOCKS[1:]):
            target = {
                "gx": lax.rem(my_x - x_offset + nx, nx),
                "gy": lax.rem(my_y + half, ny),
            }
            copies.append(
                pltpu.make_async_remote_copy(
                    src_ref=source,
                    dst_ref=landing.at[at],
                    send_sem=sems.at[0, at],
                    recv_sem=sems.at[1, at],
                    device_id=target,
                    device_id_type=MESH,
                )
            )
        return copies

    index = lax.broadcasted_iota(jnp.int32, (1, slots), 1)
    for fetch in fetches:
        fetch.wait()
    occupied = []
    for cell in range(cells):
        live = jnp.zeros((1, slots), jnp.float32)
        for tile in range(slots // tile_width):
            first = tile * tile_width
            inside = jnp.logical_and(index >= first, index < first + counts[cell, tile])
            live = jnp.where(inside, 1.0, live)
        occupied.append(live)

    for cell in range(cells):
        span = slice(cell * slots, (cell + 1) * slots)
        polar = polarity[cell : cell + 1, :]
        for m in range(3):
            stat[m : m + 1, span] = positions[m, cell : cell + 1, :]
            stat[4 + m : 5 + m, span] = dipoles[m, cell : cell + 1, :] * occupied[cell]
        stat[3:4, span] = lax.rsqrt(polar)
        stat[7:8, span] = molecules[cell : cell + 1, :].astype(jnp.float32)
        scale[0:1, span] = polar * occupied[cell]

    for stored, hist in ((past_res, res_hist), (past_out, out_hist)):
        hist[SUBLANES - 1 :, :] = jnp.zeros((1, width), jnp.float32)
        for cell in range(cells):
            for m in range(3):
                first = (cell * 3 + m) * slots
                for k in range(SUBLANES - 1):
                    row = stored[k, m, cell : cell + 1, :] * occupied[cell]
                    hist[k : k + 1, first : first + slots] = row

    wide = lax.broadcasted_iota(jnp.int32, (SUBLANES, slots), 0)
    centre = CELL_SIDE * 0.5

    def split(values):
        high = values.astype(jnp.bfloat16)
        rest = values - high.astype(jnp.float32)
        mid = rest.astype(jnp.bfloat16)
        low = (rest - mid.astype(jnp.float32)).astype(jnp.bfloat16)
        return high, mid, low

    def located(rows, x_shift, y_shift):
        shift = jnp.where(wide == 0, x_shift - centre, jnp.where(wide == 1, y_shift - cells * centre, -tiles * centre))
        moved = jnp.where(wide < 3, rows + shift, 0.0)
        return moved, jnp.sum(moved * moved, axis=0, keepdims=True)

    def in_row(at, value, rows):
        return jnp.where(wide == at, value, rows)

    turned = my_x == nx - 1
    swap = jnp.where(turned, 1, 0)

    def landing(block):
        return block - 1 if block < 2 else 2 * jnp.where(block < 4, swap, 1 - swap) + block % 2 + 1

    def arrived(landed, sems, block):
        into = landed.at[landing(block)]
        pltpu.make_async_copy(into, into, sems.at[1, landing(block)]).wait()

    def prepare(block, block_stat):
        x_offset, half = BLOCKS[block]
        x_offset = jnp.where(turned, -x_offset, x_offset).astype(jnp.float32)
        for cell in range(cells):
            rows = block_stat[:, cell * slots : (cell + 1) * slots]
            moved, norm = located(rows, CELL_SIDE * x_offset, CELL_SIDE * block_row(cell, half, cells))
            place[block, cell] = moved
            high, mid, low = (part.astype(jnp.float32) for part in split(in_row(3, norm, moved)))
            high_one, mid_one = in_row(3, 1.0, high), in_row(3, 1.0, mid)
            stack = jnp.concatenate([high, mid, high_one, low, high_one, mid_one, rows], axis=0)
            columns = jnp.transpose(stack)
            near[block, cell] = columns[:, :DEPTH].astype(jnp.bfloat16)
            spread[block, cell] = jnp.broadcast_to(columns[:, DEPTH + 3 : DEPTH + 4], (slots, LANES))
            if block == 0:
                group[cell] = jnp.broadcast_to(columns[:, DEPTH + 7 : DEPTH + 8], (slots, LANES))

    def lines(block, cell, vector):
        bx, by, bz = (place[block, cell, m : m + 1, :] for m in range(3))
        vx, vy, vz = (3.0 * v for v in vector)
        dot = bx * vx + by * vy + bz * vz
        kind = jnp.bitwise_and(wide, 3)
        right = jnp.where(kind == 0, dot, jnp.where(kind == 1, vx, jnp.where(kind == 2, vy, vz)))
        upper = wide < 4
        outer = jnp.concatenate(
            [jnp.where(upper, 1.0, bx) * right, jnp.where(upper, by, bz) * right], axis=0
        )
        ux, uy, uz = vector
        plain = jnp.concatenate(
            [in_row(4, -ux, 0.0), in_row(0, -uy, in_row(4, -uz, 0.0))], axis=0
        )
        for at, part in enumerate(zip(split(outer), split(plain))):
            for which, term in enumerate(part):
                for copy in range(2):
                    first = (2 * which + copy) * slots
                    pull[block, cell, at * TERMS : (at + 1) * TERMS, first : first + slots] = term

    def toward(target):
        rows = stat[:, target * slots : (target + 1) * slots]
        moved, norm = located(rows, 0.0, CELL_SIDE * target)
        high, mid, low = (part.astype(jnp.float32) for part in split(in_row(3, 0.0, -2.0 * moved)))
        norm_parts = [part.astype(jnp.float32) for part in split(norm + SOFTENING)]
        high_one = in_row(3, 1.0, high)
        stack = jnp.concatenate(
            [
                high_one,
                high_one,
                in_row(3, norm_parts[1], mid),
                high_one,
                in_row(3, norm_parts[2], low),
                in_row(3, norm_parts[0], mid),
            ],
            axis=0,
        )
        return stack.astype(jnp.bfloat16)

    prepare(0, stat)
    reach = [toward(c) for c in range(cells)]
    damp = [-THOLE_DAMP * stat[3:4, c * slots : (c + 1) * slots] for c in range(cells)]

    sub = lax.broadcasted_iota(jnp.int32, (SUBLANES, LANES), 0)
    lane = lax.broadcasted_iota(jnp.int32, (SUBLANES, LANES), 1)
    chunks = [slice(at * LANES, (at + 1) * LANES) for at in range(width // LANES)]

    def inner(rows, vector):
        parts = [r * v for r, v in zip(rows, vector)]
        while len(parts) > 1:
            parts = [sum(parts[at : at + 2]) for at in range(0, len(parts), 2)]
        return jnp.sum(parts[0], axis=1, keepdims=True)

    hist_rows = [res_hist[:, chunk] for chunk in chunks]
    past_gram = jnp.zeros((SUBLANES, LANES), jnp.float32)
    for k in range(SUBLANES - 1):
        column = inner(hist_rows, [rows[k : k + 1] for rows in hist_rows])
        past_gram = past_gram + jnp.where(lane == k, column, 0.0)

    met = [
        (block, cell, c, block == 0 and cell == c)
        for block in range(len(BLOCKS))
        for c in range(cells)
        for cell in range(cells)
        if (BLOCKS[block][1] == 0 or cell in (0, cells - 1))
        and abs(block_row(cell, BLOCKS[block][1], cells) - c) <= 1
    ]

    def share(mine, sent, landed, sems):
        sent[...] = mine

        def copy_to(step):
            return pltpu.make_async_remote_copy(
                src_ref=sent,
                dst_ref=landed.at[step - 1],
                send_sem=sems.at[0],
                recv_sem=sems.at[1],
                device_id=other(step),
                device_id_type=MESH,
            )

        def start():
            to_all(lambda step: copy_to(step).start())

        def finish():
            pltpu.make_async_copy(landed, landed, sems.at[1]).wait()
            return mine + jnp.sum(landed[...], axis=0)

        def sent_all():
            pltpu.make_async_copy(landed, landed, sems.at[0]).wait()

        return start, finish, sent_all

    start_past, finish_past, past_sent = share(past_gram, past_send, past_recv, past_sem)
    hist_copies = halo_copies(out_hist, hist_halo, hist_sem)

    def pair_terms(at):
        block, cell, c, same = met[at]

        def some(step, carry):
            first = pl.multiple_of(step * ROWS, ROWS)
            local = pl.ds(first, ROWS)
            s = jnp.dot(near[block, cell, local, :], reach[c], preferred_element_type=jnp.float32)
            bn = spread[block, cell, local, :]
            bn = jnp.concatenate([bn] * tiles, axis=1)
            inv = lax.rsqrt(s)
            inv2 = inv * inv
            minus_x = (s * s) * inv * (damp[c] * bn)
            e = jnp.exp(minus_x)
            t = jnp.maximum(CUTOFF_SQ - s, 0.0)
            w = t * t * (inv2 * inv)
            if same:
                mine = stat[7:8, c * slots : (c + 1) * slots]
                theirs = jnp.concatenate([group[cell, local, :]] * tiles, axis=1)
                w = jnp.where(mine != theirs, w, 0.0)
            rest = 1.0 - e
            for which, term in enumerate((w * inv2 * (rest + minus_x * e), w * rest)):
                high = term.astype(jnp.bfloat16)
                low = (term - high.astype(jnp.float32)).astype(jnp.bfloat16)
                pair[at, pl.ds(pl.multiple_of(2 * which * slots + first, ROWS), ROWS), :] = high
                pair[at, pl.ds(pl.multiple_of((2 * which + 1) * slots + first, ROWS), ROWS), :] = low
            return carry

        lax.fori_loop(0, slots // ROWS, some, 0, unroll=True)

    def pulled(at, sums):
        block, cell, c, _ = met[at]
        part = jnp.dot(pull[block, cell], pair[at], preferred_element_type=jnp.float32)
        sums[c] = part if sums[c] is None else sums[c] + part

    def jacobi_rows(sums):
        found = []
        kind = jnp.bitwise_and(wide, 3)
        for c in range(cells):
            span = slice(c * slots, (c + 1) * slots)
            ax, ay, az = (place[0, c, m : m + 1, :] for m in range(3))
            total_sum = sum(sums[c][at * TERMS : (at + 1) * TERMS] for at in range(SPLITS))
            turn = jnp.where(kind == 0, 1.0, jnp.where(kind == 1, -ax, jnp.where(kind == 2, -ay, -az)))
            folded = [total_sum[at : at + SUBLANES] * turn for at in (0, SUBLANES)]
            base, hx, hy, hz = (
                jnp.sum(jnp.where((wide < 4) == side, part, 0.0), axis=0, keepdims=True)
                for part in folded
                for side in (True, False)
            )
            for m, (h, a) in enumerate(((hx, ax), (hy, ay), (hz, az))):
                field = permanent[m, c : c + 1, :] + (h - a * base) * (1.0 / CUTOFF_SQ**2)
                row = scale[0:1, span] * field
                for tile in range(tiles):
                    found.append(row[:, tile * LANES : (tile + 1) * LANES])
        return found

    def as_row(column):
        return jnp.sum(jnp.where(sub == lane, column, 0.0), axis=0, keepdims=True)

    def mirrored(gram, row, k):
        column = jnp.sum(jnp.where(sub == lane, row, 0.0), axis=1, keepdims=True)
        return jnp.where(lane == k, column, jnp.where(sub == k, row, gram))

    def factor(gram, slot):
        rest = jnp.where(jnp.logical_or(sub == slot, lane == slot), jnp.where(sub == lane, 1.0, 0.0), gram)
        held = jnp.where(lane < SUBLANES, jnp.where(sub == lane, 1.0, 0.0), pltpu.roll(rest, SUBLANES, 1))
        for k in range(SUBLANES):
            column = jnp.broadcast_to(held[:, SUBLANES + k : SUBLANES + k + 1], held.shape)
            pivot_row = held[k : k + 1, :] / column[k : k + 1, :]
            held = jnp.where(sub == k, pivot_row, held - column * pivot_row)
        inverse = jnp.where(jnp.logical_and(lane < SUBLANES, lane != slot), held, 0.0)
        ones = jnp.sum(inverse, axis=1, keepdims=True)
        return slot, inverse, ones, as_row(ones), jnp.sum(ones, axis=0, keepdims=True)

    def solve(factored, row):
        slot, inverse, ones, ones_row, ones_sum = factored
        last = jnp.sum(jnp.where(lane[:1] == slot, row, 0.0), axis=1, keepdims=True)
        turned_row = jnp.sum(inverse * row, axis=1, keepdims=True)
        column = jnp.sum(jnp.where(jnp.logical_and(sub == lane, lane != slot), row, 0.0), axis=1, keepdims=True)
        cross = jnp.sum(ones_row * row, axis=1, keepdims=True)
        newest_y = (1.0 - cross) / (last - jnp.sum(column * turned_row, axis=0, keepdims=True))
        y = jnp.where(sub == slot, newest_y, ones - turned_row * newest_y)
        return y / (ones_sum + newest_y - cross * newest_y)

    def mixed(hist, weights, chunk):
        return jnp.sum(weights * hist, axis=0, keepdims=True)

    newest = SUBLANES - 1
    pl.semaphore_wait(barrier, total - 1)
    stat_copies = halo_copies(stat, stat_halo, stat_sem)
    for copy in stat_copies:
        copy.start()

    sums = [None] * cells
    waiting = []
    for at, blocks in enumerate(STAGES):
        for block in blocks:
            if block:
                arrived(stat_halo, stat_sem, block)
        for block in blocks:
            block_stat = stat_halo.at[landing(block)] if block else stat
            if block:
                prepare(block, block_stat)
            for cell in range(cells):
                span = slice(cell * slots, (cell + 1) * slots)
                lines(block, cell, [block_stat[4 + m : 5 + m, span] for m in range(3)])
        for one in range(len(met)):
            if met[one][0] in blocks:
                pair_terms(one)
                waiting.append(one)
                if len(waiting) > 1:
                    pulled(waiting.pop(0), sums)
        if at == len(STAGES) - 2:
            start_past()
            for copy in hist_copies:
                copy.start()
    for one in waiting:
        pulled(one, sums)

    jacobi = jacobi_rows(sums)
    for row, chunk in zip(jacobi, chunks):
        jac_own[0:1, chunk] = row
    jac_copies = halo_copies(jac_own, jac_halo, jac_sem)
    residual = []
    for at, chunk in enumerate(chunks):
        cell, rest = divmod(at, 3 * tiles)
        m, tile = divmod(rest, tiles)
        first = cell * slots + tile * LANES
        residual.append(jacobi[at] - stat[4 + m : 5 + m, first : first + LANES])
    res_rows = [jnp.where(sub == newest, r, rows) for r, rows in zip(residual, hist_rows)]
    row = as_row(inner(res_rows, residual))
    start, finish, first_sent = share(row, row_send.at[0], row_recv.at[0], row_sem.at[0])
    for copy in jac_copies:
        copy.start()
    start()
    past_gram = finish_past()
    factored = factor(past_gram, newest)
    row = finish()
    weights = solve(factored, row)
    gram = mirrored(past_gram, row, newest)

    current = []
    for at, chunk in enumerate(chunks):
        row = mixed(out_hist[:, chunk], weights, chunk) + weights[newest : newest + 1] * jacobi[at]
        current.append(row)
        vec[0:1, chunk] = row
    for block in range(1, len(BLOCKS)):
        arrived(hist_halo, hist_sem, block)
        arrived(jac_halo, jac_sem, block)
        for chunk in chunks:
            vec[block : block + 1, chunk] = (
                mixed(hist_halo[landing(block), :, chunk], weights, chunk)
                + weights[newest : newest + 1] * jac_halo[landing(block), 0:1, chunk]
            )
    for block in range(len(BLOCKS)):
        for cell in range(cells):
            starts = [(cell * 3 + m) * slots for m in range(3)]
            lines(block, cell, [vec[block : block + 1, at : at + slots] for at in starts])
    sums = [None] * cells
    for at in range(len(met)):
        pulled(at, sums)

    jacobi_next = jacobi_rows(sums)
    residual = [a - b for a, b in zip(jacobi_next, current)]
    res_rows = [jnp.where(sub == 0, r, rows) for r, rows in zip(residual, res_rows)]
    row = as_row(inner(res_rows, residual))
    start, finish, second_sent = share(row, row_send.at[1], row_recv.at[1], row_sem.at[1])
    start()
    factored = factor(gram, 0)
    weights = solve(factored, finish())
    kept = jnp.where(sub == 0, 0.0, weights)
    for at, chunk in enumerate(chunks):
        cell, rest = divmod(at, 3 * tiles)
        m, tile = divmod(rest, tiles)
        next_ref[0, m, cell : cell + 1, tile * LANES : (tile + 1) * LANES] = (
            mixed(out_hist[:, chunk], kept, chunk)
            + weights[newest : newest + 1] * jac_own[0:1, chunk]
            + weights[0:1] * jacobi_next[at]
        )
    column = jnp.concatenate([weights[1:], weights[0:1]], axis=0)
    weight_ref[...] = as_row(column)[0, :SUBLANES]

    for copy in stat_copies + hist_copies + jac_copies:
        copy.wait_send()
    past_sent()
    first_sent()
    second_sent()


def wired(arg_count, nx, ny, cells, slots, tile_width, counts_arg, *refs):
    args, rest = refs[:arg_count], refs[arg_count:]
    outs, rest = rest[:2], rest[2:]
    held, rest = rest[:arg_count], rest[arg_count:]
    counts, *rest = rest
    args, inside = (*args, counts_arg), (*held, counts)
    kernel(nx, ny, cells, slots, tile_width, args, outs, inside, *rest)


def body(nx, ny, positions, polarizability, tile_counts, molecules, perm_field, dipoles, past_out, past_res):
    cells, tile_count = tile_counts.shape[1:]
    slots = positions.shape[-1]
    tile_width = slots // tile_count
    tiles = slots // LANES
    past = past_out.shape[2]
    assert ny == 2 and nx > 2 and cells > 1 and past + 1 == SUBLANES and slots % LANES == 0
    width = cells * 3 * slots

    halo = len(BLOCKS) - 1
    met = 3 * (3 * cells)
    vmem = pl.BlockSpec(memory_space=pltpu.VMEM)
    hbm = pl.BlockSpec(memory_space=pltpu.HBM)
    raw = (
        jnp.swapaxes(positions, 1, 2),
        polarizability,
        molecules,
        jnp.swapaxes(perm_field, 1, 2),
        jnp.swapaxes(dipoles, 1, 2),
        jnp.transpose(past_out, (0, 2, 3, 1, 4)),
        jnp.transpose(past_res, (0, 2, 3, 1, 4)),
    )
    tile_counts, *raw = (
        pltpu.with_memory_space_constraint(arg, pltpu.HBM) for arg in (tile_counts, *raw)
    )
    pairs_kept = met * slots * slots
    current, weights = pl.pallas_call(
        functools.partial(wired, len(raw), nx, ny, cells, slots, tile_width),
        out_shape=(
            jax.ShapeDtypeStruct((1, 3, cells, slots), jnp.float32),
            jax.ShapeDtypeStruct((SUBLANES,), jnp.float32),
        ),
        in_specs=[hbm] * (1 + len(raw)),
        out_specs=(vmem, vmem),
        scratch_shapes=[pltpu.VMEM(arg.shape[1:], arg.dtype) for arg in raw]
        + [
            pltpu.SMEM(tile_counts.shape[1:], tile_counts.dtype),
            pltpu.VMEM((SUBLANES, cells * slots), jnp.float32),
            pltpu.VMEM((SUBLANES, width), jnp.float32),
            pltpu.VMEM((SUBLANES, width), jnp.float32),
            pltpu.VMEM((1, cells * slots), jnp.float32),
            pltpu.VMEM((halo, SUBLANES, cells * slots), jnp.float32),
            pltpu.VMEM((halo, SUBLANES, width), jnp.float32),
            pltpu.VMEM((halo, 1, width), jnp.float32),
            pltpu.VMEM((halo + 1, cells, SUBLANES, slots), jnp.float32),
            pltpu.VMEM((halo + 1, cells, slots, DEPTH), jnp.bfloat16),
            pltpu.VMEM((halo + 1, cells, slots, LANES), jnp.float32),
            pltpu.VMEM((cells, slots, LANES), jnp.float32),
            pltpu.VMEM((halo + 1, cells, SPLITS * TERMS, 4 * slots), jnp.bfloat16),
            pltpu.VMEM((met, 4 * slots, slots), jnp.bfloat16),
            pltpu.VMEM((1, width), jnp.float32),
            pltpu.VMEM((SUBLANES, width), jnp.float32),
            pltpu.VMEM((SUBLANES, LANES), jnp.float32),
            pltpu.VMEM((nx * ny - 1, SUBLANES, LANES), jnp.float32),
            pltpu.VMEM((2, 1, LANES), jnp.float32),
            pltpu.VMEM((2, nx * ny - 1, 1, LANES), jnp.float32),
            pltpu.SemaphoreType.DMA((len(raw) + 1,)),
            pltpu.SemaphoreType.DMA((2, halo)),
            pltpu.SemaphoreType.DMA((2, halo)),
            pltpu.SemaphoreType.DMA((2, halo)),
            pltpu.SemaphoreType.DMA((2,)),
            pltpu.SemaphoreType.DMA((2, 2)),
        ],
        compiler_params=pltpu.CompilerParams(
            collective_id=0, has_side_effects=True, vmem_limit_bytes=32 * 1024 * 1024
        ),
        cost_estimate=pl.CostEstimate(
            flops=70 * pairs_kept, bytes_accessed=16 * width * SUBLANES, transcendentals=2 * pairs_kept
        ),
    )(tile_counts, *raw)
    return (jnp.swapaxes(current, 1, 2), weights)


def solution(mesh):
    cell_axes = P(("box", "gx"), "gy")
    return jax.shard_map(
        functools.partial(body, mesh.shape["gx"], mesh.shape["gy"]),
        mesh=mesh,
        in_specs=(cell_axes,) * 8,
        out_specs=(cell_axes, P("box")),
        check_vma=False,
    )
```

```python
import functools

import jax
import jax.numpy as jnp
from jax import lax
from jax.experimental import pallas as pl
from jax.experimental.pallas import tpu as pltpu
from jax.sharding import PartitionSpec as P

CELL_SIDE = 9.0
CUTOFF_SQ = 81.0
SOFTENING = 0.25
THOLE_DAMP = 0.39
LANES = 128
SUBLANES = 8
ROWS = 32
DEPTH = 48
SPLITS = 3
TERMS = 16
MESH = pl.DeviceIdType.MESH

HIST_AT = 1
STAGES = ((0,), (1,), (2, 3), (4, 5))
BLOCKS = ((0, 0), (0, 1), (1, 0), (1, 1), (-1, 0), (-1, 1))


def block_row(cell, half, cells):
    if half == 0:
        return cell
    return -1 if cell == cells - 1 else cells


def kernel(
    nx,
    ny,
    cells,
    slots,
    tile_width,
    args,
    outs,
    held,
    stat,
    out_hist,
    res_hist,
    scale,
    stat_halo,
    hist_halo,
    jac_halo,
    place,
    near,
    spread,
    group,
    pull,
    pair,
    jac_own,
    vec,
    past_send,
    past_recv,
    row_send,
    row_recv,
    in_sem,
    stat_sem,
    hist_sem,
    jac_sem,
    past_sem,
    row_sem,
):
    next_ref, weight_ref = outs
    positions, polarity, molecules, permanent, dipoles, past_out, past_res, counts = held
    tiles = slots // LANES
    width = cells * 3 * slots
    total = nx * ny
    my_x = lax.axis_index("gx")
    my_y = lax.axis_index("gy")

    barrier = pltpu.get_barrier_semaphore()
    fetches = [
        pltpu.make_async_copy(arg.at[0], into, in_sem.at[at])
        for at, (arg, into) in enumerate(zip(args, held))
    ]
    for fetch in fetches:
        fetch.start()

    few = total <= 2 * SUBLANES

    def to_all(act):
        def both(step, carry):
            for ahead in (step, nx - step):
                column = my_x + ahead
                column = jnp.where(column >= nx, column - nx, column)
                for across in range(ny):
                    act(ahead * ny + across - 1, {"gx": column, "gy": jnp.where(my_y + across >= ny, 0, my_y + across)})
            return carry

        lax.fori_loop(1, nx // 2, both, 0, unroll=few)
        column = jnp.where(my_x >= nx // 2, my_x - nx // 2, my_x + nx // 2)
        for across in range(ny):
            act(nx // 2 * ny + across - 1, {"gx": column, "gy": jnp.where(my_y + across >= ny, 0, my_y + across)})
        act(0, {"gx": my_x, "gy": 1 - my_y})

    def greet(slot, target):
        pl.semaphore_signal(barrier, inc=1, device_id=target, device_id_type=MESH)

    to_all(greet)

    def halo_copies(source, landing, sems):
        copies = []
        for at, (x_offset, half) in enumerate(BLOCKS[1:]):
            target = {
                "gx": lax.rem(my_x - x_offset + nx, nx),
                "gy": lax.rem(my_y + half, ny),
            }
            copies.append(
                pltpu.make_async_remote_copy(
                    src_ref=source,
                    dst_ref=landing.at[at],
                    send_sem=sems.at[0, at],
                    recv_sem=sems.at[1, at],
                    device_id=target,
                    device_id_type=MESH,
                )
            )
        return copies

    index = lax.broadcasted_iota(jnp.int32, (1, slots), 1)
    for fetch in fetches:
        fetch.wait()
    occupied = []
    for cell in range(cells):
        live = jnp.zeros((1, slots), jnp.float32)
        for tile in range(slots // tile_width):
            first = tile * tile_width
            inside = jnp.logical_and(index >= first, index < first + counts[cell, tile])
            live = jnp.where(inside, 1.0, live)
        occupied.append(live)

    for cell in range(cells):
        span = slice(cell * slots, (cell + 1) * slots)
        polar = polarity[cell : cell + 1, :]
        for m in range(3):
            stat[m : m + 1, span] = positions[m, cell : cell + 1, :]
            stat[4 + m : 5 + m, span] = dipoles[m, cell : cell + 1, :] * occupied[cell]
        stat[3:4, span] = lax.rsqrt(polar)
        stat[7:8, span] = molecules[cell : cell + 1, :].astype(jnp.float32)
        scale[0:1, span] = polar * occupied[cell]

    for stored, hist in ((past_res, res_hist), (past_out, out_hist)):
        hist[SUBLANES - 1 :, :] = jnp.zeros((1, width), jnp.float32)
        for cell in range(cells):
            for m in range(3):
                first = (cell * 3 + m) * slots
                for k in range(SUBLANES - 1):
                    row = stored[k, m, cell : cell + 1, :] * occupied[cell]
                    hist[k : k + 1, first : first + slots] = row

    wide = lax.broadcasted_iota(jnp.int32, (SUBLANES, slots), 0)
    centre = CELL_SIDE * 0.5

    def split(values):
        high = values.astype(jnp.bfloat16)
        rest = values - high.astype(jnp.float32)
        mid = rest.astype(jnp.bfloat16)
        low = (rest - mid.astype(jnp.float32)).astype(jnp.bfloat16)
        return high, mid, low

    def located(rows, x_shift, y_shift):
        shift = jnp.where(wide == 0, x_shift - centre, jnp.where(wide == 1, y_shift - cells * centre, -tiles * centre))
        moved = jnp.where(wide < 3, rows + shift, 0.0)
        return moved, jnp.sum(moved * moved, axis=0, keepdims=True)

    def in_row(at, value, rows):
        return jnp.where(wide == at, value, rows)

    turned = my_x == nx - 1
    swap = jnp.where(turned, 1, 0)

    def landing(block):
        return block - 1 if block < 2 else 2 * jnp.where(block < 4, swap, 1 - swap) + block % 2 + 1

    def arrived(landed, sems, block):
        into = landed.at[landing(block)]
        pltpu.make_async_copy(into, into, sems.at[1, landing(block)]).wait()

    def prepare(block, block_stat):
        x_offset, half = BLOCKS[block]
        x_offset = jnp.where(turned, -x_offset, x_offset).astype(jnp.float32)
        for cell in range(cells):
            rows = block_stat[:, cell * slots : (cell + 1) * slots]
            moved, norm = located(rows, CELL_SIDE * x_offset, CELL_SIDE * block_row(cell, half, cells))
            place[block, cell] = moved
            high, mid, low = (part.astype(jnp.float32) for part in split(in_row(3, norm, moved)))
            high_one, mid_one = in_row(3, 1.0, high), in_row(3, 1.0, mid)
            stack = jnp.concatenate([high, mid, high_one, low, high_one, mid_one, rows], axis=0)
            columns = jnp.transpose(stack)
            near[block, cell] = columns[:, :DEPTH].astype(jnp.bfloat16)
            spread[block, cell] = jnp.broadcast_to(columns[:, DEPTH + 3 : DEPTH + 4], (slots, LANES))
            if block == 0:
                group[cell] = jnp.broadcast_to(columns[:, DEPTH + 7 : DEPTH + 8], (slots, LANES))

    def lines(block, cell, vector):
        bx, by, bz = (place[block, cell, m : m + 1, :] for m in range(3))
        vx, vy, vz = (3.0 * v for v in vector)
        dot = bx * vx + by * vy + bz * vz
        kind = jnp.bitwise_and(wide, 3)
        right = jnp.where(kind == 0, dot, jnp.where(kind == 1, vx, jnp.where(kind == 2, vy, vz)))
        upper = wide < 4
        outer = jnp.concatenate(
            [jnp.where(upper, 1.0, bx) * right, jnp.where(upper, by, bz) * right], axis=0
        )
        ux, uy, uz = vector
        plain = jnp.concatenate(
            [in_row(4, -ux, 0.0), in_row(0, -uy, in_row(4, -uz, 0.0))], axis=0
        )
        for at, part in enumerate(zip(split(outer), split(plain))):
            for which, term in enumerate(part):
                for copy in range(2):
                    first = (2 * which + copy) * slots
                    pull[block, cell, at * TERMS : (at + 1) * TERMS, first : first + slots] = term

    def toward(target):
        rows = stat[:, target * slots : (target + 1) * slots]
        moved, norm = located(rows, 0.0, CELL_SIDE * target)
        high, mid, low = (part.astype(jnp.float32) for part in split(in_row(3, 0.0, -2.0 * moved)))
        norm_parts = [part.astype(jnp.float32) for part in split(norm + SOFTENING)]
        high_one = in_row(3, 1.0, high)
        stack = jnp.concatenate(
            [
                high_one,
                high_one,
                in_row(3, norm_parts[1], mid),
                high_one,
                in_row(3, norm_parts[2], low),
                in_row(3, norm_parts[0], mid),
            ],
            axis=0,
        )
        return stack.astype(jnp.bfloat16)

    prepare(0, stat)
    reach = [toward(c) for c in range(cells)]
    damp = [-THOLE_DAMP * stat[3:4, c * slots : (c + 1) * slots] for c in range(cells)]

    sub = lax.broadcasted_iota(jnp.int32, (SUBLANES, LANES), 0)
    lane = lax.broadcasted_iota(jnp.int32, (SUBLANES, LANES), 1)
    chunks = [slice(at * LANES, (at + 1) * LANES) for at in range(width // LANES)]

    def inner(rows, vector):
        parts = [r * v for r, v in zip(rows, vector)]
        while len(parts) > 1:
            parts = [sum(parts[at : at + 2]) for at in range(0, len(parts), 2)]
        return jnp.sum(parts[0], axis=1, keepdims=True)

    hist_rows = [res_hist[:, chunk] for chunk in chunks]
    past_gram = jnp.zeros((SUBLANES, LANES), jnp.float32)
    for k in range(SUBLANES - 1):
        column = inner(hist_rows, [rows[k : k + 1] for rows in hist_rows])
        past_gram = past_gram + jnp.where(lane == k, column, 0.0)

    met = [
        (block, cell, c, block == 0 and cell == c)
        for block in range(len(BLOCKS))
        for c in range(cells)
        for cell in range(cells)
        if (BLOCKS[block][1] == 0 or cell in (0, cells - 1))
        and abs(block_row(cell, BLOCKS[block][1], cells) - c) <= 1
    ]

    def share(mine, sent, landed, sems):
        sent[...] = mine

        def send(slot, target):
            pltpu.make_async_remote_copy(
                src_ref=sent,
                dst_ref=landed.at[slot],
                send_sem=sems.at[0],
                recv_sem=sems.at[1],
                device_id=target,
                device_id_type=MESH,
            ).start()

        def start():
            to_all(send)

        def finish():
            pltpu.make_async_copy(landed, landed, sems.at[1]).wait()
            return mine + jnp.sum(landed[...], axis=0)

        def sent_all():
            pltpu.make_async_copy(landed, landed, sems.at[0]).wait()

        return start, finish, sent_all

    start_past, finish_past, past_sent = share(past_gram, past_send, past_recv, past_sem)
    hist_copies = [
        copy for at, copy in enumerate(halo_copies(out_hist, hist_halo, hist_sem)) if at == 0 or at % 2
    ]
    handed = [
        pltpu.make_async_remote_copy(
            src_ref=hist_halo.at[at],
            dst_ref=hist_halo.at[at + 1],
            send_sem=hist_sem.at[0, at + 1],
            recv_sem=hist_sem.at[1, at + 1],
            device_id={"gx": my_x, "gy": 1 - my_y},
            device_id_type=MESH,
        )
        for at in range(1, len(BLOCKS) - 1, 2)
    ]

    def pair_terms(at):
        block, cell, c, same = met[at]

        def some(step, carry):
            first = pl.multiple_of(step * ROWS, ROWS)
            local = pl.ds(first, ROWS)
            s = jnp.dot(near[block, cell, local, :], reach[c], preferred_element_type=jnp.float32)
            bn = spread[block, cell, local, :]
            bn = jnp.concatenate([bn] * tiles, axis=1)
            inv = lax.rsqrt(s)
            inv2 = inv * inv
            minus_x = (s * s) * inv * (damp[c] * bn)
            e = jnp.exp(minus_x)
            t = jnp.maximum(CUTOFF_SQ - s, 0.0)
            w = t * t * (inv2 * inv)
            if same:
                mine = stat[7:8, c * slots : (c + 1) * slots]
                theirs = jnp.concatenate([group[cell, local, :]] * tiles, axis=1)
                w = jnp.where(mine != theirs, w, 0.0)
            rest = 1.0 - e
            for which, term in enumerate((w * inv2 * (rest + minus_x * e), w * rest)):
                high = term.astype(jnp.bfloat16)
                low = (term - high.astype(jnp.float32)).astype(jnp.bfloat16)
                pair[at, pl.ds(pl.multiple_of(2 * which * slots + first, ROWS), ROWS), :] = high
                pair[at, pl.ds(pl.multiple_of((2 * which + 1) * slots + first, ROWS), ROWS), :] = low
            return carry

        lax.fori_loop(0, slots // ROWS, some, 0, unroll=True)

    def pulled(at, sums):
        block, cell, c, _ = met[at]
        part = jnp.dot(pull[block, cell], pair[at], preferred_element_type=jnp.float32)
        sums[c] = part if sums[c] is None else sums[c] + part

    def jacobi_rows(sums):
        found = []
        kind = jnp.bitwise_and(wide, 3)
        for c in range(cells):
            span = slice(c * slots, (c + 1) * slots)
            ax, ay, az = (place[0, c, m : m + 1, :] for m in range(3))
            total_sum = sum(sums[c][at * TERMS : (at + 1) * TERMS] for at in range(SPLITS))
            turn = jnp.where(kind == 0, 1.0, jnp.where(kind == 1, -ax, jnp.where(kind == 2, -ay, -az)))
            folded = [total_sum[at : at + SUBLANES] * turn for at in (0, SUBLANES)]
            base, hx, hy, hz = (
                jnp.sum(jnp.where((wide < 4) == side, part, 0.0), axis=0, keepdims=True)
                for part in folded
                for side in (True, False)
            )
            for m, (h, a) in enumerate(((hx, ax), (hy, ay), (hz, az))):
                field = permanent[m, c : c + 1, :] + (h - a * base) * (1.0 / CUTOFF_SQ**2)
                row = scale[0:1, span] * field
                for tile in range(tiles):
                    found.append(row[:, tile * LANES : (tile + 1) * LANES])
        return found

    def as_row(column):
        return jnp.sum(jnp.where(sub == lane, column, 0.0), axis=0, keepdims=True)

    def mirrored(gram, row, k):
        column = jnp.sum(jnp.where(sub == lane, row, 0.0), axis=1, keepdims=True)
        return jnp.where(lane == k, column, jnp.where(sub == k, row, gram))

    def factor(gram, slot):
        rest = jnp.where(jnp.logical_or(sub == slot, lane == slot), jnp.where(sub == lane, 1.0, 0.0), gram)
        held = jnp.where(lane < SUBLANES, jnp.where(sub == lane, 1.0, 0.0), pltpu.roll(rest, SUBLANES, 1))
        for k in range(SUBLANES):
            column = jnp.broadcast_to(held[:, SUBLANES + k : SUBLANES + k + 1], held.shape)
            pivot_row = held[k : k + 1, :] / column[k : k + 1, :]
            held = jnp.where(sub == k, pivot_row, held - column * pivot_row)
        inverse = jnp.where(jnp.logical_and(lane < SUBLANES, lane != slot), held, 0.0)
        ones = jnp.sum(inverse, axis=1, keepdims=True)
        return slot, inverse, ones, as_row(ones), jnp.sum(ones, axis=0, keepdims=True)

    def solve(factored, row):
        slot, inverse, ones, ones_row, ones_sum = factored
        last = jnp.sum(jnp.where(lane[:1] == slot, row, 0.0), axis=1, keepdims=True)
        turned_row = jnp.sum(inverse * row, axis=1, keepdims=True)
        column = jnp.sum(jnp.where(jnp.logical_and(sub == lane, lane != slot), row, 0.0), axis=1, keepdims=True)
        cross = jnp.sum(ones_row * row, axis=1, keepdims=True)
        newest_y = (1.0 - cross) / (last - jnp.sum(column * turned_row, axis=0, keepdims=True))
        y = jnp.where(sub == slot, newest_y, ones - turned_row * newest_y)
        return y / (ones_sum + newest_y - cross * newest_y)

    def mixed(hist, weights, chunk):
        return jnp.sum(weights * hist, axis=0, keepdims=True)

    newest = SUBLANES - 1
    pl.semaphore_wait(barrier, total - 1)
    stat_copies = halo_copies(stat, stat_halo, stat_sem)
    for copy in stat_copies:
        copy.start()

    sums = [None] * cells
    waiting = []
    for at, blocks in enumerate(STAGES):
        for block in blocks:
            if block:
                arrived(stat_halo, stat_sem, block)
        for block in blocks:
            block_stat = stat_halo.at[landing(block)] if block else stat
            if block:
                prepare(block, block_stat)
            for cell in range(cells):
                span = slice(cell * slots, (cell + 1) * slots)
                lines(block, cell, [block_stat[4 + m : 5 + m, span] for m in range(3)])
        for one in range(len(met)):
            if met[one][0] in blocks:
                pair_terms(one)
                waiting.append(one)
                if len(waiting) > 1:
                    pulled(waiting.pop(0), sums)
        if at == HIST_AT:
            start_past()
            for copy in hist_copies:
                copy.start()
    for one in waiting:
        pulled(one, sums)

    jacobi = jacobi_rows(sums)
    for row, chunk in zip(jacobi, chunks):
        jac_own[0:1, chunk] = row
    jac_copies = halo_copies(jac_own, jac_halo, jac_sem)
    residual = []
    for at, chunk in enumerate(chunks):
        cell, rest = divmod(at, 3 * tiles)
        m, tile = divmod(rest, tiles)
        first = cell * slots + tile * LANES
        residual.append(jacobi[at] - stat[4 + m : 5 + m, first : first + LANES])
    res_rows = [jnp.where(sub == newest, r, rows) for r, rows in zip(residual, hist_rows)]
    row = as_row(inner(res_rows, residual))
    start, finish, first_sent = share(row, row_send.at[0], row_recv.at[0], row_sem.at[0])
    for copy in jac_copies:
        copy.start()
    start()
    for copy, hand in zip(hist_copies[1:], handed):
        copy.wait_recv()
        hand.start()
    past_gram = finish_past()
    factored = factor(past_gram, newest)
    row = finish()
    weights = solve(factored, row)
    gram = mirrored(past_gram, row, newest)

    current = []
    for at, chunk in enumerate(chunks):
        row = mixed(out_hist[:, chunk], weights, chunk) + weights[newest : newest + 1] * jacobi[at]
        current.append(row)
        vec[0:1, chunk] = row
    for block in range(1, len(BLOCKS)):
        if BLOCKS[block][1]:
            arrived(hist_halo, hist_sem, block)
        arrived(jac_halo, jac_sem, block)
        for chunk in chunks:
            vec[block : block + 1, chunk] = (
                mixed(hist_halo[landing(block), :, chunk], weights, chunk)
                + weights[newest : newest + 1] * jac_halo[landing(block), 0:1, chunk]
            )
    for block in range(len(BLOCKS)):
        for cell in range(cells):
            starts = [(cell * 3 + m) * slots for m in range(3)]
            lines(block, cell, [vec[block : block + 1, at : at + slots] for at in starts])
    sums = [None] * cells
    for at in range(len(met)):
        pulled(at, sums)

    jacobi_next = jacobi_rows(sums)
    residual = [a - b for a, b in zip(jacobi_next, current)]
    res_rows = [jnp.where(sub == 0, r, rows) for r, rows in zip(residual, res_rows)]
    row = as_row(inner(res_rows, residual))
    start, finish, second_sent = share(row, row_send.at[1], row_recv.at[1], row_sem.at[1])
    start()
    factored = factor(gram, 0)
    weights = solve(factored, finish())
    kept = jnp.where(sub == 0, 0.0, weights)
    for at, chunk in enumerate(chunks):
        cell, rest = divmod(at, 3 * tiles)
        m, tile = divmod(rest, tiles)
        next_ref[0, m, cell : cell + 1, tile * LANES : (tile + 1) * LANES] = (
            mixed(out_hist[:, chunk], kept, chunk)
            + weights[newest : newest + 1] * jac_own[0:1, chunk]
            + weights[0:1] * jacobi_next[at]
        )
    column = jnp.concatenate([weights[1:], weights[0:1]], axis=0)
    weight_ref[...] = as_row(column)[0, :SUBLANES]

    for copy in stat_copies + hist_copies + handed + jac_copies:
        copy.wait_send()
    past_sent()
    first_sent()
    second_sent()


def wired(arg_count, nx, ny, cells, slots, tile_width, counts_arg, *refs):
    args, rest = refs[:arg_count], refs[arg_count:]
    outs, rest = rest[:2], rest[2:]
    held, rest = rest[:arg_count], rest[arg_count:]
    counts, *rest = rest
    args, inside = (*args, counts_arg), (*held, counts)
    kernel(nx, ny, cells, slots, tile_width, args, outs, inside, *rest)


def body(nx, ny, positions, polarizability, tile_counts, molecules, perm_field, dipoles, past_out, past_res):
    cells, tile_count = tile_counts.shape[1:]
    slots = positions.shape[-1]
    tile_width = slots // tile_count
    tiles = slots // LANES
    past = past_out.shape[2]
    assert ny == 2 and nx > 2 and cells > 1 and past + 1 == SUBLANES and slots % LANES == 0
    width = cells * 3 * slots

    halo = len(BLOCKS) - 1
    met = 3 * (3 * cells)
    vmem = pl.BlockSpec(memory_space=pltpu.VMEM)
    hbm = pl.BlockSpec(memory_space=pltpu.HBM)
    raw = (
        jnp.swapaxes(positions, 1, 2),
        polarizability,
        molecules,
        jnp.swapaxes(perm_field, 1, 2),
        jnp.swapaxes(dipoles, 1, 2),
        jnp.transpose(past_out, (0, 2, 3, 1, 4)),
        jnp.transpose(past_res, (0, 2, 3, 1, 4)),
    )
    tile_counts, *raw = (
        pltpu.with_memory_space_constraint(arg, pltpu.HBM) for arg in (tile_counts, *raw)
    )
    pairs_kept = met * slots * slots
    current, weights = pl.pallas_call(
        functools.partial(wired, len(raw), nx, ny, cells, slots, tile_width),
        out_shape=(
            jax.ShapeDtypeStruct((1, 3, cells, slots), jnp.float32),
            jax.ShapeDtypeStruct((SUBLANES,), jnp.float32),
        ),
        in_specs=[hbm] * (1 + len(raw)),
        out_specs=(vmem, vmem),
        scratch_shapes=[pltpu.VMEM(arg.shape[1:], arg.dtype) for arg in raw]
        + [
            pltpu.SMEM(tile_counts.shape[1:], tile_counts.dtype),
            pltpu.VMEM((SUBLANES, cells * slots), jnp.float32),
            pltpu.VMEM((SUBLANES, width), jnp.float32),
            pltpu.VMEM((SUBLANES, width), jnp.float32),
            pltpu.VMEM((1, cells * slots), jnp.float32),
            pltpu.VMEM((halo, SUBLANES, cells * slots), jnp.float32),
            pltpu.VMEM((halo, SUBLANES, width), jnp.float32),
            pltpu.VMEM((halo, 1, width), jnp.float32),
            pltpu.VMEM((halo + 1, cells, SUBLANES, slots), jnp.float32),
            pltpu.VMEM((halo + 1, cells, slots, DEPTH), jnp.bfloat16),
            pltpu.VMEM((halo + 1, cells, slots, LANES), jnp.float32),
            pltpu.VMEM((cells, slots, LANES), jnp.float32),
            pltpu.VMEM((halo + 1, cells, SPLITS * TERMS, 4 * slots), jnp.bfloat16),
            pltpu.VMEM((met, 4 * slots, slots), jnp.bfloat16),
            pltpu.VMEM((1, width), jnp.float32),
            pltpu.VMEM((SUBLANES, width), jnp.float32),
            pltpu.VMEM((SUBLANES, LANES), jnp.float32),
            pltpu.VMEM((nx * ny - 1, SUBLANES, LANES), jnp.float32),
            pltpu.VMEM((2, 1, LANES), jnp.float32),
            pltpu.VMEM((2, nx * ny - 1, 1, LANES), jnp.float32),
            pltpu.SemaphoreType.DMA((len(raw) + 1,)),
            pltpu.SemaphoreType.DMA((2, halo)),
            pltpu.SemaphoreType.DMA((2, halo)),
            pltpu.SemaphoreType.DMA((2, halo)),
            pltpu.SemaphoreType.DMA((2,)),
            pltpu.SemaphoreType.DMA((2, 2)),
        ],
        compiler_params=pltpu.CompilerParams(
            collective_id=0, has_side_effects=True, vmem_limit_bytes=32 * 1024 * 1024
        ),
        cost_estimate=pl.CostEstimate(
            flops=70 * pairs_kept, bytes_accessed=16 * width * SUBLANES, transcendentals=2 * pairs_kept
        ),
    )(tile_counts, *raw)
    return (jnp.swapaxes(current, 1, 2), weights)


def solution(mesh):
    cell_axes = P(("box", "gx"), "gy")
    return jax.shard_map(
        functools.partial(body, mesh.shape["gx"], mesh.shape["gy"]),
        mesh=mesh,
        in_specs=(cell_axes,) * 8,
        out_specs=(cell_axes, P("box")),
        check_vma=False,
    )
```

```python
import functools

import jax
import jax.numpy as jnp
from jax import lax
from jax.experimental import pallas as pl
from jax.experimental.pallas import tpu as pltpu
from jax.sharding import PartitionSpec as P

CELL_SIDE = 9.0
CUTOFF_SQ = 81.0
SOFTENING = 0.25
THOLE_DAMP = 0.39
LANES = 128
SUBLANES = 8
ROWS = 32
DEPTH = 48
SPLITS = 3
TERMS = 16
MESH = pl.DeviceIdType.MESH

HIST_AT = 1
STAGES = ((0,), (1,), (2, 3), (4, 5))
BLOCKS = ((0, 0), (0, 1), (1, 0), (1, 1), (-1, 0), (-1, 1))


def block_row(cell, half, cells):
    if half == 0:
        return cell
    return -1 if cell == cells - 1 else cells


def kernel(
    nx,
    ny,
    cells,
    slots,
    tile_width,
    args,
    outs,
    held,
    stat,
    out_hist,
    res_hist,
    scale,
    stat_halo,
    hist_halo,
    jac_halo,
    place,
    near,
    group,
    pull,
    pair,
    stored_pull,
    stored_iso,
    stored_acc,
    stored_iso_acc,
    stored_field,
    jac_own,
    past_send,
    past_recv,
    row_send,
    row_recv,
    in_sem,
    stat_sem,
    hist_sem,
    jac_sem,
    past_sem,
    row_sem,
):
    next_ref, weight_ref = outs
    positions, polarity, molecules, permanent, dipoles, past_out, past_res, counts = held
    tiles = slots // LANES
    width = cells * 3 * slots
    total = nx * ny
    my_x = lax.axis_index("gx")
    my_y = lax.axis_index("gy")

    barrier = pltpu.get_barrier_semaphore()
    fetches = [
        pltpu.make_async_copy(arg.at[0], into, in_sem.at[at])
        for at, (arg, into) in enumerate(zip(args, held))
    ]
    for fetch in fetches:
        fetch.start()

    few = total <= 2 * SUBLANES

    def to_all(act):
        def both(step, carry):
            for ahead in (step, nx - step):
                column = my_x + ahead
                column = jnp.where(column >= nx, column - nx, column)
                for across in range(ny):
                    act(ahead * ny + across - 1, {"gx": column, "gy": jnp.where(my_y + across >= ny, 0, my_y + across)})
            return carry

        lax.fori_loop(1, nx // 2, both, 0, unroll=few)
        column = jnp.where(my_x >= nx // 2, my_x - nx // 2, my_x + nx // 2)
        for across in range(ny):
            act(nx // 2 * ny + across - 1, {"gx": column, "gy": jnp.where(my_y + across >= ny, 0, my_y + across)})
        act(0, {"gx": my_x, "gy": 1 - my_y})

    def greet(slot, target):
        pl.semaphore_signal(barrier, inc=1, device_id=target, device_id_type=MESH)

    to_all(greet)

    def halo_copies(source, landing, sems):
        copies = []
        for at, (x_offset, half) in enumerate(BLOCKS[1:]):
            target = {
                "gx": lax.rem(my_x - x_offset + nx, nx),
                "gy": lax.rem(my_y + half, ny),
            }
            copies.append(
                pltpu.make_async_remote_copy(
                    src_ref=source,
                    dst_ref=landing.at[at],
                    send_sem=sems.at[0, at],
                    recv_sem=sems.at[1, at],
                    device_id=target,
                    device_id_type=MESH,
                )
            )
        return copies

    index = lax.broadcasted_iota(jnp.int32, (1, slots), 1)
    for fetch in fetches:
        fetch.wait()
    occupied = []
    for cell in range(cells):
        live = jnp.zeros((1, slots), jnp.float32)
        for tile in range(slots // tile_width):
            first = tile * tile_width
            inside = jnp.logical_and(index >= first, index < first + counts[cell, tile])
            live = jnp.where(inside, 1.0, live)
        occupied.append(live)

    for cell in range(cells):
        span = slice(cell * slots, (cell + 1) * slots)
        polar = polarity[cell : cell + 1, :]
        for m in range(3):
            stat[m : m + 1, span] = positions[m, cell : cell + 1, :]
            stat[4 + m : 5 + m, span] = dipoles[m, cell : cell + 1, :] * occupied[cell]
        stat[3:4, span] = lax.rsqrt(polar)
        stat[7:8, span] = molecules[cell : cell + 1, :].astype(jnp.float32)
        scale[0:1, span] = polar * occupied[cell]

    for stored, hist in ((past_res, res_hist), (past_out, out_hist)):
        hist[SUBLANES - 1 :, :] = jnp.zeros((1, width), jnp.float32)
        for cell in range(cells):
            for m in range(3):
                first = (cell * 3 + m) * slots
                for k in range(SUBLANES - 1):
                    row = stored[k, m, cell : cell + 1, :] * occupied[cell]
                    hist[k : k + 1, first : first + slots] = row

    wide = lax.broadcasted_iota(jnp.int32, (SUBLANES, slots), 0)
    centre = CELL_SIDE * 0.5

    def split(values):
        high = values.astype(jnp.bfloat16)
        rest = values - high.astype(jnp.float32)
        mid = rest.astype(jnp.bfloat16)
        low = (rest - mid.astype(jnp.float32)).astype(jnp.bfloat16)
        return high, mid, low

    def located(rows, x_shift, y_shift):
        shift = jnp.where(wide == 0, x_shift - centre, jnp.where(wide == 1, y_shift - cells * centre, -tiles * centre))
        moved = jnp.where(wide < 3, rows + shift, 0.0)
        return moved, jnp.sum(moved * moved, axis=0, keepdims=True)

    def in_row(at, value, rows):
        return jnp.where(wide == at, value, rows)

    turned = my_x == nx - 1
    swap = jnp.where(turned, 1, 0)

    def landing(block):
        return block - 1 if block < 2 else 2 * jnp.where(block < 4, swap, 1 - swap) + block % 2 + 1

    def arrived(landed, sems, block):
        into = landed.at[landing(block)]
        pltpu.make_async_copy(into, into, sems.at[1, landing(block)]).wait()

    def prepare(block, block_stat):
        x_offset, half = BLOCKS[block]
        x_offset = jnp.where(turned, -x_offset, x_offset).astype(jnp.float32)
        for cell in range(cells):
            rows = block_stat[:, cell * slots : (cell + 1) * slots]
            moved, norm = located(rows, CELL_SIDE * x_offset, CELL_SIDE * block_row(cell, half, cells))
            place[block, cell] = moved
            sides = in_row(3, 1.0, in_row(4, norm, moved))
            stack = []
            for values in (sides, sides * rows[3:4, :]):
                high, mid, low = (part.astype(jnp.float32) for part in split(values))
                stack += [high, mid, high, low, high, mid]
            if block == 0:
                stack.append(rows)
            columns = jnp.transpose(jnp.concatenate(stack, axis=0))
            near[block, cell] = columns[:, : 2 * DEPTH].astype(jnp.bfloat16)
            if block == 0:
                group[cell] = jnp.broadcast_to(columns[:, 2 * DEPTH + 7 : 2 * DEPTH + 8], (slots, LANES))

    def lines(block, cell, vector):
        bx, by, bz = (place[block, cell, m : m + 1, :] for m in range(3))
        vx, vy, vz = (3.0 * v for v in vector)
        dot = bx * vx + by * vy + bz * vz
        kind = jnp.bitwise_and(wide, 3)
        right = jnp.where(kind == 0, dot, jnp.where(kind == 1, vx, jnp.where(kind == 2, vy, vz)))
        upper = wide < 4
        outer = jnp.concatenate(
            [jnp.where(upper, 1.0, bx) * right, jnp.where(upper, by, bz) * right], axis=0
        )
        ux, uy, uz = vector
        plain = jnp.concatenate(
            [in_row(4, -ux, 0.0), in_row(0, -uy, in_row(4, -uz, 0.0))], axis=0
        )
        for at, part in enumerate(zip(split(outer), split(plain))):
            for which, term in enumerate(part):
                for copy in range(2):
                    first = (2 * which + copy) * slots
                    pull[block, cell, at * TERMS : (at + 1) * TERMS, first : first + slots] = term

    def stored_lines(block, cell, hist):
        bx, by, bz = (place[block, cell, m : m + 1, :] for m in range(3))
        plain = [hist[:, (cell * 3 + m) * slots : (cell * 3 + m + 1) * slots] for m in range(3)]
        vx, vy, vz = (3.0 * v for v in plain)
        right = (bx * vx + by * vy + bz * vz, vx, vy, vz)
        outer = [r if left is None else left * r for left in (None, bx, by, bz) for r in right]
        for into, rows in ((stored_pull, outer), (stored_iso, [-v for v in plain])):
            values = jnp.concatenate(rows, axis=0)
            high, mid, _ = split(values)
            both = jnp.concatenate([high.astype(jnp.float32), mid.astype(jnp.float32)], axis=0)
            both = both.astype(jnp.bfloat16)
            for copy in range(2):
                into[block, cell, :, copy * slots : (copy + 1) * slots] = both

    def stored_pulled(at, begun):
        block, cell, c, _ = met[at]
        for left, acc, first in ((stored_pull, stored_acc, 0), (stored_iso, stored_iso_acc, 2 * slots)):
            part = jnp.dot(
                left[block, cell], pair[at, first : first + 2 * slots, :], preferred_element_type=jnp.float32
            )
            acc[c] = acc[c] + part if c in begun else part
        begun.add(c)

    def stored_fields():
        for c in range(cells):
            ax, ay, az = (place[0, c, m : m + 1, :] for m in range(3))

            def term(at):
                first, second = at * SUBLANES, (TERMS + at) * SUBLANES
                return stored_acc[c, first : first + SUBLANES, :] + stored_acc[c, second : second + SUBLANES, :]

            base, hx, hy, hz = (
                term(4 * i) - ax * term(4 * i + 1) - ay * term(4 * i + 2) - az * term(4 * i + 3) for i in range(4)
            )
            for m, (h, a) in enumerate(((hx, ax), (hy, ay), (hz, az))):
                first, second = m * SUBLANES, (3 + m) * SUBLANES
                iso = stored_iso_acc[c, first : first + SUBLANES, :] + stored_iso_acc[c, second : second + SUBLANES, :]
                stored_field[:, (c * 3 + m) * slots : (c * 3 + m + 1) * slots] = h - a * base + iso

    def toward(target):
        rows = stat[:, target * slots : (target + 1) * slots]
        moved, norm = located(rows, 0.0, CELL_SIDE * target)
        norm = norm + SOFTENING
        sides = in_row(3, norm, in_row(4, 1.0, -2.0 * moved))
        blank = jnp.zeros((DEPTH, slots), jnp.bfloat16)
        columns = []
        for values, first in (
            (sides, True),
            (sides * (-THOLE_DAMP * rows[3:4, :]), False),
            (in_row(3, CUTOFF_SQ - norm, -sides), True),
        ):
            high, mid, low = (part.astype(jnp.float32) for part in split(values))
            part = jnp.concatenate([high, high, mid, high, low, mid], axis=0).astype(jnp.bfloat16)
            columns.append(jnp.concatenate([part, blank] if first else [blank, part], axis=0))
        return jnp.concatenate(columns, axis=1)

    prepare(0, stat)
    reach = [toward(c) for c in range(cells)]

    sub = lax.broadcasted_iota(jnp.int32, (SUBLANES, LANES), 0)
    lane = lax.broadcasted_iota(jnp.int32, (SUBLANES, LANES), 1)
    chunks = [slice(at * LANES, (at + 1) * LANES) for at in range(width // LANES)]

    def inner(rows, vector):
        parts = [r * v for r, v in zip(rows, vector)]
        while len(parts) > 1:
            parts = [sum(parts[at : at + 2]) for at in range(0, len(parts), 2)]
        return jnp.sum(parts[0], axis=1, keepdims=True)

    hist_rows = [res_hist[:, chunk] for chunk in chunks]
    past_gram = jnp.zeros((SUBLANES, LANES), jnp.float32)
    for k in range(SUBLANES - 1):
        column = inner(hist_rows, [rows[k : k + 1] for rows in hist_rows])
        past_gram = past_gram + jnp.where(lane == k, column, 0.0)

    met = [
        (block, cell, c, block == 0 and cell == c)
        for block in range(len(BLOCKS))
        for c in range(cells)
        for cell in range(cells)
        if (BLOCKS[block][1] == 0 or cell in (0, cells - 1))
        and abs(block_row(cell, BLOCKS[block][1], cells) - c) <= 1
    ]

    def share(mine, sent, landed, sems):
        sent[...] = mine

        def send(slot, target):
            pltpu.make_async_remote_copy(
                src_ref=sent,
                dst_ref=landed.at[slot],
                send_sem=sems.at[0],
                recv_sem=sems.at[1],
                device_id=target,
                device_id_type=MESH,
            ).start()

        def start():
            to_all(send)

        def finish():
            pltpu.make_async_copy(landed, landed, sems.at[1]).wait()
            return mine + jnp.sum(landed[...], axis=0)

        def sent_all():
            pltpu.make_async_copy(landed, landed, sems.at[0]).wait()

        return start, finish, sent_all

    start_past, finish_past, past_sent = share(past_gram, past_send, past_recv, past_sem)
    hist_copies = [
        copy for at, copy in enumerate(halo_copies(out_hist, hist_halo, hist_sem)) if at == 0 or at % 2
    ]
    handed = [
        pltpu.make_async_remote_copy(
            src_ref=hist_halo.at[landing(block)],
            dst_ref=hist_halo.at[landing(block) + 1],
            send_sem=hist_sem.at[0, landing(block) + 1],
            recv_sem=hist_sem.at[1, landing(block) + 1],
            device_id={"gx": my_x, "gy": 1 - my_y},
            device_id_type=MESH,
        )
        for block in range(2, len(BLOCKS), 2)
    ]

    def pair_terms(at):
        block, cell, c, same = met[at]

        def some(step, carry):
            first = pl.multiple_of(step * ROWS, ROWS)
            local = pl.ds(first, ROWS)
            found = jnp.dot(near[block, cell, local, :], reach[c], preferred_element_type=jnp.float32)
            s, scaled, left = (found[:, at * slots : (at + 1) * slots] for at in range(3))
            inv = lax.rsqrt(s)
            minus_x = scaled * (s * inv)
            e = jnp.exp(minus_x)
            t = jnp.maximum(left, 0.0) * inv
            w = t * t * inv
            if same:
                mine = stat[7:8, c * slots : (c + 1) * slots]
                theirs = jnp.concatenate([group[cell, local, :]] * tiles, axis=1)
                w = jnp.where(mine != theirs, w, 0.0)
            rest = 1.0 - e
            for which, term in enumerate((w * (inv * inv) * (rest + minus_x * e), w * rest)):
                high = term.astype(jnp.bfloat16)
                low = (term - high.astype(jnp.float32)).astype(jnp.bfloat16)
                pair[at, pl.ds(pl.multiple_of(2 * which * slots + first, ROWS), ROWS), :] = high
                pair[at, pl.ds(pl.multiple_of((2 * which + 1) * slots + first, ROWS), ROWS), :] = low
            return carry

        lax.fori_loop(0, slots // ROWS, some, 0, unroll=True)

    def pulled(at, sums):
        block, cell, c, _ = met[at]
        part = jnp.dot(pull[block, cell], pair[at], preferred_element_type=jnp.float32)
        sums[c] = part if sums[c] is None else sums[c] + part

    def field_rows(sums):
        found = []
        kind = jnp.bitwise_and(wide, 3)
        for c in range(cells):
            ax, ay, az = (place[0, c, m : m + 1, :] for m in range(3))
            total_sum = sum(sums[c][at * TERMS : (at + 1) * TERMS] for at in range(SPLITS))
            turn = jnp.where(kind == 0, 1.0, jnp.where(kind == 1, -ax, jnp.where(kind == 2, -ay, -az)))
            folded = [total_sum[at : at + SUBLANES] * turn for at in (0, SUBLANES)]
            base, hx, hy, hz = (
                jnp.sum(jnp.where((wide < 4) == side, part, 0.0), axis=0, keepdims=True)
                for part in folded
                for side in (True, False)
            )
            for m, (h, a) in enumerate(((hx, ax), (hy, ay), (hz, az))):
                row = h - a * base
                for tile in range(tiles):
                    found.append(row[:, tile * LANES : (tile + 1) * LANES])
        return found

    def jacobi_rows(fields):
        found = []
        for at, field in enumerate(fields):
            cell, m, tile, first = whereabouts(at)
            whole = permanent[m, cell : cell + 1, tile * LANES : (tile + 1) * LANES] + field * (1.0 / CUTOFF_SQ**2)
            found.append(scale[0:1, first : first + LANES] * whole)
        return found

    def whereabouts(at):
        cell, rest = divmod(at, 3 * tiles)
        m, tile = divmod(rest, tiles)
        return cell, m, tile, cell * slots + tile * LANES

    def as_row(column):
        return jnp.sum(jnp.where(sub == lane, column, 0.0), axis=0, keepdims=True)

    def mirrored(gram, row, k):
        column = jnp.sum(jnp.where(sub == lane, row, 0.0), axis=1, keepdims=True)
        return jnp.where(lane == k, column, jnp.where(sub == k, row, gram))

    def factor(gram, slot):
        rest = jnp.where(jnp.logical_or(sub == slot, lane == slot), jnp.where(sub == lane, 1.0, 0.0), gram)
        held = jnp.where(lane < SUBLANES, jnp.where(sub == lane, 1.0, 0.0), pltpu.roll(rest, SUBLANES, 1))
        for k in range(SUBLANES):
            column = jnp.broadcast_to(held[:, SUBLANES + k : SUBLANES + k + 1], held.shape)
            pivot_row = held[k : k + 1, :] / column[k : k + 1, :]
            held = jnp.where(sub == k, pivot_row, held - column * pivot_row)
        inverse = jnp.where(jnp.logical_and(lane < SUBLANES, lane != slot), held, 0.0)
        ones = jnp.sum(inverse, axis=1, keepdims=True)
        return slot, inverse, ones, as_row(ones), jnp.sum(ones, axis=0, keepdims=True)

    def solve(factored, row):
        slot, inverse, ones, ones_row, ones_sum = factored
        last = jnp.sum(jnp.where(lane[:1] == slot, row, 0.0), axis=1, keepdims=True)
        turned_row = jnp.sum(inverse * row, axis=1, keepdims=True)
        column = jnp.sum(jnp.where(jnp.logical_and(sub == lane, lane != slot), row, 0.0), axis=1, keepdims=True)
        cross = jnp.sum(ones_row * row, axis=1, keepdims=True)
        newest_y = (1.0 - cross) / (last - jnp.sum(column * turned_row, axis=0, keepdims=True))
        y = jnp.where(sub == slot, newest_y, ones - turned_row * newest_y)
        return y / (ones_sum + newest_y - cross * newest_y)

    def mixed(hist, weights, chunk):
        return jnp.sum(weights * hist, axis=0, keepdims=True)

    newest = SUBLANES - 1
    pl.semaphore_wait(barrier, total - 1)
    stat_copies = halo_copies(stat, stat_halo, stat_sem)
    for copy in stat_copies:
        copy.start()

    sums = [None] * cells
    waiting = []
    for at, blocks in enumerate(STAGES):
        for block in blocks:
            if block:
                arrived(stat_halo, stat_sem, block)
        for block in blocks:
            block_stat = stat_halo.at[landing(block)] if block else stat
            if block:
                prepare(block, block_stat)
            for cell in range(cells):
                span = slice(cell * slots, (cell + 1) * slots)
                lines(block, cell, [block_stat[4 + m : 5 + m, span] for m in range(3)])
        for one in range(len(met)):
            if met[one][0] in blocks:
                pair_terms(one)
                waiting.append(one)
                if len(waiting) > 1:
                    pulled(waiting.pop(0), sums)
        if at == HIST_AT:
            start_past()
            for copy in hist_copies:
                copy.start()
    for one in waiting:
        pulled(one, sums)

    jacobi = jacobi_rows(field_rows(sums))
    for row, chunk in zip(jacobi, chunks):
        jac_own[0:1, chunk] = row
    jac_copies = halo_copies(jac_own, jac_halo, jac_sem)
    residual = []
    for at, chunk in enumerate(chunks):
        cell, rest = divmod(at, 3 * tiles)
        m, tile = divmod(rest, tiles)
        first = cell * slots + tile * LANES
        residual.append(jacobi[at] - stat[4 + m : 5 + m, first : first + LANES])
    res_rows = [jnp.where(sub == newest, r, rows) for r, rows in zip(residual, hist_rows)]
    row = as_row(inner(res_rows, residual))
    start, finish, first_sent = share(row, row_send.at[0], row_recv.at[0], row_sem.at[0])
    for copy in jac_copies:
        copy.start()
    start()
    begun = set()
    sums = [None] * cells

    def hand_on(block):
        arrived(hist_halo, hist_sem, block)
        handed[block // 2 - 1].start()

    def met_in(block):
        return [at for at in range(len(met)) if met[at][0] == block]

    def stored_stage(block):
        if block % 2:
            arrived(hist_halo, hist_sem, block)
        hist = hist_halo.at[landing(block)] if block else out_hist
        for cell in range(cells):
            stored_lines(block, cell, hist)
        for at in met_in(block):
            stored_pulled(at, begun)

    def jacobi_stage(block):
        source = jac_halo.at[landing(block)] if block else jac_own
        for cell in range(cells):
            starts = [(cell * 3 + m) * slots for m in range(3)]
            lines(block, cell, [source[0:1, at : at + slots] for at in starts])
        for at in met_in(block):
            pulled(at, sums)

    hand_on(2)
    stored_stage(0)
    jacobi_stage(0)
    stored_stage(1)
    hand_on(4)
    past_gram = finish_past()
    factored = factor(past_gram, newest)
    stored_stage(2)
    arrived(jac_halo, jac_sem, 1)
    jacobi_stage(1)
    stored_stage(3)
    stored_stage(4)
    arrived(jac_halo, jac_sem, 2)
    arrived(jac_halo, jac_sem, 3)
    jacobi_stage(2)
    jacobi_stage(3)
    stored_stage(5)
    stored_fields()
    arrived(jac_halo, jac_sem, 4)
    arrived(jac_halo, jac_sem, 5)
    row = finish()
    jacobi_stage(4)
    jacobi_stage(5)
    weights = solve(factored, row)
    gram = mirrored(past_gram, row, newest)
    fields = [
        mixed(stored_field[:, chunk], weights, chunk) + weights[newest : newest + 1] * field
        for chunk, field in zip(chunks, field_rows(sums))
    ]
    current = [
        mixed(out_hist[:, chunk], weights, chunk) + weights[newest : newest + 1] * row
        for chunk, row in zip(chunks, jacobi)
    ]
    jacobi_next = jacobi_rows(fields)
    residual = [a - b for a, b in zip(jacobi_next, current)]
    res_rows = [jnp.where(sub == 0, r, rows) for r, rows in zip(residual, res_rows)]
    row = as_row(inner(res_rows, residual))
    start, finish, second_sent = share(row, row_send.at[1], row_recv.at[1], row_sem.at[1])
    start()
    factored = factor(gram, 0)
    weights = solve(factored, finish())
    kept = jnp.where(sub == 0, 0.0, weights)
    for at, chunk in enumerate(chunks):
        cell, rest = divmod(at, 3 * tiles)
        m, tile = divmod(rest, tiles)
        next_ref[0, m, cell : cell + 1, tile * LANES : (tile + 1) * LANES] = (
            mixed(out_hist[:, chunk], kept, chunk)
            + weights[newest : newest + 1] * jac_own[0:1, chunk]
            + weights[0:1] * jacobi_next[at]
        )
    column = jnp.concatenate([weights[1:], weights[0:1]], axis=0)
    weight_ref[...] = as_row(column)[0, :SUBLANES]

    for copy in stat_copies + hist_copies + handed + jac_copies:
        copy.wait_send()
    past_sent()
    first_sent()
    second_sent()


def wired(arg_count, nx, ny, cells, slots, tile_width, counts_arg, *refs):
    args, rest = refs[:arg_count], refs[arg_count:]
    outs, rest = rest[:2], rest[2:]
    held, rest = rest[:arg_count], rest[arg_count:]
    counts, *rest = rest
    args, inside = (*args, counts_arg), (*held, counts)
    kernel(nx, ny, cells, slots, tile_width, args, outs, inside, *rest)


def body(nx, ny, positions, polarizability, tile_counts, molecules, perm_field, dipoles, past_out, past_res):
    cells, tile_count = tile_counts.shape[1:]
    slots = positions.shape[-1]
    tile_width = slots // tile_count
    tiles = slots // LANES
    past = past_out.shape[2]
    assert ny == 2 and nx > 2 and cells > 1 and past + 1 == SUBLANES and slots % LANES == 0
    width = cells * 3 * slots

    halo = len(BLOCKS) - 1
    met = 3 * (3 * cells)
    vmem = pl.BlockSpec(memory_space=pltpu.VMEM)
    hbm = pl.BlockSpec(memory_space=pltpu.HBM)
    raw = (
        jnp.swapaxes(positions, 1, 2),
        polarizability,
        molecules,
        jnp.swapaxes(perm_field, 1, 2),
        jnp.swapaxes(dipoles, 1, 2),
        jnp.transpose(past_out, (0, 2, 3, 1, 4)),
        jnp.transpose(past_res, (0, 2, 3, 1, 4)),
    )
    tile_counts, *raw = (
        pltpu.with_memory_space_constraint(arg, pltpu.HBM) for arg in (tile_counts, *raw)
    )
    pairs_kept = met * slots * slots
    current, weights = pl.pallas_call(
        functools.partial(wired, len(raw), nx, ny, cells, slots, tile_width),
        out_shape=(
            jax.ShapeDtypeStruct((1, 3, cells, slots), jnp.float32),
            jax.ShapeDtypeStruct((SUBLANES,), jnp.float32),
        ),
        in_specs=[hbm] * (1 + len(raw)),
        out_specs=(vmem, vmem),
        scratch_shapes=[pltpu.VMEM(arg.shape[1:], arg.dtype) for arg in raw]
        + [
            pltpu.SMEM(tile_counts.shape[1:], tile_counts.dtype),
            pltpu.VMEM((SUBLANES, cells * slots), jnp.float32),
            pltpu.VMEM((SUBLANES, width), jnp.float32),
            pltpu.VMEM((SUBLANES, width), jnp.float32),
            pltpu.VMEM((1, cells * slots), jnp.float32),
            pltpu.VMEM((halo, SUBLANES, cells * slots), jnp.float32),
            pltpu.VMEM((halo, SUBLANES, width), jnp.float32),
            pltpu.VMEM((halo, 1, width), jnp.float32),
            pltpu.VMEM((halo + 1, cells, SUBLANES, slots), jnp.float32),
            pltpu.VMEM((halo + 1, cells, slots, 2 * DEPTH), jnp.bfloat16),
            pltpu.VMEM((cells, slots, LANES), jnp.float32),
            pltpu.VMEM((halo + 1, cells, SPLITS * TERMS, 4 * slots), jnp.bfloat16),
            pltpu.VMEM((met, 4 * slots, slots), jnp.bfloat16),
            pltpu.VMEM((halo + 1, cells, 2 * TERMS * SUBLANES, 2 * slots), jnp.bfloat16),
            pltpu.VMEM((halo + 1, cells, 2 * 3 * SUBLANES, 2 * slots), jnp.bfloat16),
            pltpu.VMEM((cells, 2 * TERMS * SUBLANES, slots), jnp.float32),
            pltpu.VMEM((cells, 2 * 3 * SUBLANES, slots), jnp.float32),
            pltpu.VMEM((SUBLANES, width), jnp.float32),
            pltpu.VMEM((1, width), jnp.float32),
            pltpu.VMEM((SUBLANES, LANES), jnp.float32),
            pltpu.VMEM((nx * ny - 1, SUBLANES, LANES), jnp.float32),
            pltpu.VMEM((2, 1, LANES), jnp.float32),
            pltpu.VMEM((2, nx * ny - 1, 1, LANES), jnp.float32),
            pltpu.SemaphoreType.DMA((len(raw) + 1,)),
            pltpu.SemaphoreType.DMA((2, halo)),
            pltpu.SemaphoreType.DMA((2, halo)),
            pltpu.SemaphoreType.DMA((2, halo)),
            pltpu.SemaphoreType.DMA((2,)),
            pltpu.SemaphoreType.DMA((2, 2)),
        ],
        compiler_params=pltpu.CompilerParams(
            collective_id=0, has_side_effects=True, vmem_limit_bytes=32 * 1024 * 1024
        ),
        cost_estimate=pl.CostEstimate(
            flops=70 * pairs_kept, bytes_accessed=16 * width * SUBLANES, transcendentals=2 * pairs_kept
        ),
    )(tile_counts, *raw)
    return (jnp.swapaxes(current, 1, 2), weights)


def solution(mesh):
    cell_axes = P(("box", "gx"), "gy")
    return jax.shard_map(
        functools.partial(body, mesh.shape["gx"], mesh.shape["gy"]),
        mesh=mesh,
        in_specs=(cell_axes,) * 8,
        out_specs=(cell_axes, P("box")),
        check_vma=False,
    )
```

```python
import functools

import jax
import jax.numpy as jnp
from jax import lax
from jax.experimental import pallas as pl
from jax.experimental.pallas import tpu as pltpu
from jax.sharding import PartitionSpec as P

CELL_SIDE = 9.0
CUTOFF_SQ = 81.0
SOFTENING = 0.25
THOLE_DAMP = 0.39
LANES = 128
SUBLANES = 8
ROWS = 32
DEPTH = 48
SPLITS = 3
TERMS = 16
MESH = pl.DeviceIdType.MESH

HIST_AT = 1
STAGES = ((0,), (1,), (2, 3), (4, 5))
BLOCKS = ((0, 0), (0, 1), (1, 0), (1, 1), (-1, 0), (-1, 1))


def block_row(cell, half, cells):
    if half == 0:
        return cell
    return -1 if cell == cells - 1 else cells


def kernel(
    nx,
    ny,
    cells,
    slots,
    tile_width,
    args,
    outs,
    held,
    stat,
    out_hist,
    res_hist,
    scale,
    stat_halo,
    hist_halo,
    jac_halo,
    place,
    near,
    group,
    pull,
    pair,
    stored_pull,
    stored_iso,
    stored_acc,
    stored_iso_acc,
    stored_field,
    jac_own,
    past_send,
    past_recv,
    row_send,
    row_recv,
    in_sem,
    stat_sem,
    hist_sem,
    jac_sem,
    past_sem,
    row_sem,
):
    next_ref, weight_ref = outs
    positions, polarity, molecules, permanent, dipoles, past_out, past_res, counts = held
    tiles = slots // LANES
    width = cells * 3 * slots
    total = nx * ny
    my_x = lax.axis_index("gx")
    my_y = lax.axis_index("gy")

    barrier = pltpu.get_barrier_semaphore()
    fetches = [
        pltpu.make_async_copy(arg.at[0], into, in_sem.at[at])
        for at, (arg, into) in enumerate(zip(args, held))
    ]
    for fetch in fetches:
        fetch.start()

    few = total <= 2 * SUBLANES

    def to_all(act):
        def both(step, carry):
            for ahead in (step, nx - step):
                column = my_x + ahead
                column = jnp.where(column >= nx, column - nx, column)
                for across in range(ny):
                    act(ahead * ny + across - 1, {"gx": column, "gy": jnp.where(my_y + across >= ny, 0, my_y + across)})
            return carry

        lax.fori_loop(1, nx // 2, both, 0, unroll=few)
        column = jnp.where(my_x >= nx // 2, my_x - nx // 2, my_x + nx // 2)
        for across in range(ny):
            act(nx // 2 * ny + across - 1, {"gx": column, "gy": jnp.where(my_y + across >= ny, 0, my_y + across)})
        act(0, {"gx": my_x, "gy": 1 - my_y})

    def greet(slot, target):
        pl.semaphore_signal(barrier, inc=1, device_id=target, device_id_type=MESH)

    to_all(greet)

    def halo_copies(source, landing, sems):
        copies = []
        for at, (x_offset, half) in enumerate(BLOCKS[1:]):
            target = {
                "gx": lax.rem(my_x - x_offset + nx, nx),
                "gy": lax.rem(my_y + half, ny),
            }
            copies.append(
                pltpu.make_async_remote_copy(
                    src_ref=source,
                    dst_ref=landing.at[at],
                    send_sem=sems.at[0, at],
                    recv_sem=sems.at[1, at],
                    device_id=target,
                    device_id_type=MESH,
                )
            )
        return copies

    index = lax.broadcasted_iota(jnp.int32, (1, slots), 1)
    for fetch in fetches:
        fetch.wait()
    occupied = []
    for cell in range(cells):
        live = jnp.zeros((1, slots), jnp.float32)
        for tile in range(slots // tile_width):
            first = tile * tile_width
            inside = jnp.logical_and(index >= first, index < first + counts[cell, tile])
            live = jnp.where(inside, 1.0, live)
        occupied.append(live)

    for cell in range(cells):
        span = slice(cell * slots, (cell + 1) * slots)
        polar = polarity[cell : cell + 1, :]
        for m in range(3):
            stat[m : m + 1, span] = positions[m, cell : cell + 1, :]
            stat[4 + m : 5 + m, span] = dipoles[m, cell : cell + 1, :] * occupied[cell]
        stat[3:4, span] = lax.rsqrt(polar)
        stat[7:8, span] = molecules[cell : cell + 1, :].astype(jnp.float32)
        scale[0:1, span] = polar * occupied[cell]

    for stored, hist in ((past_res, res_hist), (past_out, out_hist)):
        hist[SUBLANES - 1 :, :] = jnp.zeros((1, width), jnp.float32)
        for cell in range(cells):
            for m in range(3):
                first = (cell * 3 + m) * slots
                for k in range(SUBLANES - 1):
                    row = stored[k, m, cell : cell + 1, :] * occupied[cell]
                    hist[k : k + 1, first : first + slots] = row

    wide = lax.broadcasted_iota(jnp.int32, (SUBLANES, slots), 0)
    centre = CELL_SIDE * 0.5

    def split(values):
        high = values.astype(jnp.bfloat16)
        rest = values - high.astype(jnp.float32)
        mid = rest.astype(jnp.bfloat16)
        low = (rest - mid.astype(jnp.float32)).astype(jnp.bfloat16)
        return high, mid, low

    def located(rows, x_shift, y_shift):
        shift = jnp.where(wide == 0, x_shift - centre, jnp.where(wide == 1, y_shift - cells * centre, -tiles * centre))
        moved = jnp.where(wide < 3, rows + shift, 0.0)
        return moved, jnp.sum(moved * moved, axis=0, keepdims=True)

    def in_row(at, value, rows):
        return jnp.where(wide == at, value, rows)

    turned = my_x == nx - 1
    swap = jnp.where(turned, 1, 0)

    def landing(block):
        return block - 1 if block < 2 else 2 * jnp.where(block < 4, swap, 1 - swap) + block % 2 + 1

    def arrived(landed, sems, block):
        into = landed.at[landing(block)]
        pltpu.make_async_copy(into, into, sems.at[1, landing(block)]).wait()

    def prepare(block, block_stat):
        x_offset, half = BLOCKS[block]
        x_offset = jnp.where(turned, -x_offset, x_offset).astype(jnp.float32)
        for cell in range(cells):
            rows = block_stat[:, cell * slots : (cell + 1) * slots]
            moved, norm = located(rows, CELL_SIDE * x_offset, CELL_SIDE * block_row(cell, half, cells))
            place[block, cell] = moved
            sides = in_row(3, 1.0, in_row(4, norm, moved))
            stack = []
            for values in (sides, sides * rows[3:4, :]):
                high, mid, low = (part.astype(jnp.float32) for part in split(values))
                stack += [high, mid, high, low, high, mid]
            if block == 0:
                stack.append(rows)
            columns = jnp.transpose(jnp.concatenate(stack, axis=0))
            near[block, cell] = columns[:, : 2 * DEPTH].astype(jnp.bfloat16)
            if block == 0:
                group[cell] = jnp.broadcast_to(columns[:, 2 * DEPTH + 7 : 2 * DEPTH + 8], (slots, LANES))

    def lines(block, cell, vector):
        bx, by, bz = (place[block, cell, m : m + 1, :] for m in range(3))
        vx, vy, vz = (3.0 * v for v in vector)
        dot = bx * vx + by * vy + bz * vz
        kind = jnp.bitwise_and(wide, 3)
        right = jnp.where(kind == 0, dot, jnp.where(kind == 1, vx, jnp.where(kind == 2, vy, vz)))
        upper = wide < 4
        outer = jnp.concatenate(
            [jnp.where(upper, 1.0, bx) * right, jnp.where(upper, by, bz) * right], axis=0
        )
        ux, uy, uz = vector
        plain = jnp.concatenate(
            [in_row(4, -ux, 0.0), in_row(0, -uy, in_row(4, -uz, 0.0))], axis=0
        )
        for at, part in enumerate(zip(split(outer), split(plain))):
            for which, term in enumerate(part):
                for copy in range(2):
                    first = (2 * which + copy) * slots
                    pull[block, cell, at * TERMS : (at + 1) * TERMS, first : first + slots] = term

    def stored_lines(block, cell, hist):
        bx, by, bz = (place[block, cell, m : m + 1, :] for m in range(3))
        plain = [hist[:, (cell * 3 + m) * slots : (cell * 3 + m + 1) * slots] for m in range(3)]
        vx, vy, vz = (3.0 * v for v in plain)
        right = (bx * vx + by * vy + bz * vz, vx, vy, vz)
        outer = [r if left is None else left * r for left in (None, bx, by, bz) for r in right]
        for into, rows in ((stored_pull, outer), (stored_iso, [-v for v in plain])):
            values = jnp.concatenate(rows, axis=0)
            high, mid, _ = split(values)
            both = jnp.concatenate([high.astype(jnp.float32), mid.astype(jnp.float32)], axis=0)
            both = both.astype(jnp.bfloat16)
            for copy in range(2):
                into[block, cell, :, copy * slots : (copy + 1) * slots] = both

    def stored_pulled(at, begun):
        block, cell, c, _ = met[at]
        for left, acc, first in ((stored_pull, stored_acc, 0), (stored_iso, stored_iso_acc, 2 * slots)):
            part = jnp.dot(
                left[block, cell], pair[at, first : first + 2 * slots, :], preferred_element_type=jnp.float32
            )
            acc[c] = acc[c] + part if c in begun else part
        begun.add(c)

    def stored_fields():
        for c in range(cells):
            ax, ay, az = (place[0, c, m : m + 1, :] for m in range(3))

            def term(at):
                first, second = at * SUBLANES, (TERMS + at) * SUBLANES
                return stored_acc[c, first : first + SUBLANES, :] + stored_acc[c, second : second + SUBLANES, :]

            base, hx, hy, hz = (
                term(4 * i) - ax * term(4 * i + 1) - ay * term(4 * i + 2) - az * term(4 * i + 3) for i in range(4)
            )
            for m, (h, a) in enumerate(((hx, ax), (hy, ay), (hz, az))):
                first, second = m * SUBLANES, (3 + m) * SUBLANES
                iso = stored_iso_acc[c, first : first + SUBLANES, :] + stored_iso_acc[c, second : second + SUBLANES, :]
                stored_field[:, (c * 3 + m) * slots : (c * 3 + m + 1) * slots] = h - a * base + iso

    def toward(target):
        rows = stat[:, target * slots : (target + 1) * slots]
        moved, norm = located(rows, 0.0, CELL_SIDE * target)
        norm = norm + SOFTENING
        sides = in_row(3, norm, in_row(4, 1.0, -2.0 * moved))
        blank = jnp.zeros((DEPTH, slots), jnp.bfloat16)
        columns = []
        for values, first in (
            (sides, True),
            (sides * (-THOLE_DAMP * rows[3:4, :]), False),
            (in_row(3, CUTOFF_SQ - norm, -sides), True),
        ):
            high, mid, low = (part.astype(jnp.float32) for part in split(values))
            part = jnp.concatenate([high, high, mid, high, low, mid], axis=0).astype(jnp.bfloat16)
            columns.append(jnp.concatenate([part, blank] if first else [blank, part], axis=0))
        return jnp.concatenate(columns, axis=1)

    prepare(0, stat)
    reach = [toward(c) for c in range(cells)]

    sub = lax.broadcasted_iota(jnp.int32, (SUBLANES, LANES), 0)
    lane = lax.broadcasted_iota(jnp.int32, (SUBLANES, LANES), 1)
    chunks = [slice(at * LANES, (at + 1) * LANES) for at in range(width // LANES)]

    def inner(rows, vector):
        parts = [r * v for r, v in zip(rows, vector)]
        while len(parts) > 1:
            parts = [sum(parts[at : at + 2]) for at in range(0, len(parts), 2)]
        return jnp.sum(parts[0], axis=1, keepdims=True)

    hist_rows = [res_hist[:, chunk] for chunk in chunks]
    past_gram = jnp.zeros((SUBLANES, LANES), jnp.float32)
    for k in range(SUBLANES - 1):
        column = inner(hist_rows, [rows[k : k + 1] for rows in hist_rows])
        past_gram = past_gram + jnp.where(lane == k, column, 0.0)

    met = [
        (block, cell, c, block == 0 and cell == c)
        for block in range(len(BLOCKS))
        for c in range(cells)
        for cell in range(cells)
        if (BLOCKS[block][1] == 0 or cell in (0, cells - 1))
        and abs(block_row(cell, BLOCKS[block][1], cells) - c) <= 1
    ]

    def share(mine, sent, landed, sems):
        sent[...] = mine

        def send(slot, target):
            pltpu.make_async_remote_copy(
                src_ref=sent,
                dst_ref=landed.at[slot],
                send_sem=sems.at[0],
                recv_sem=sems.at[1],
                device_id=target,
                device_id_type=MESH,
            ).start()

        def start():
            to_all(send)

        def finish():
            pltpu.make_async_copy(landed, landed, sems.at[1]).wait()
            return mine + jnp.sum(landed[...], axis=0)

        def sent_all():
            pltpu.make_async_copy(landed, landed, sems.at[0]).wait()

        return start, finish, sent_all

    start_past, finish_past, past_sent = share(past_gram, past_send, past_recv, past_sem)
    hist_copies = [
        copy for at, copy in enumerate(halo_copies(out_hist, hist_halo, hist_sem)) if at == 0 or at % 2
    ]
    handed = [
        pltpu.make_async_remote_copy(
            src_ref=hist_halo.at[landing(block)],
            dst_ref=hist_halo.at[landing(block) + 1],
            send_sem=hist_sem.at[0, landing(block) + 1],
            recv_sem=hist_sem.at[1, landing(block) + 1],
            device_id={"gx": my_x, "gy": 1 - my_y},
            device_id_type=MESH,
        )
        for block in range(2, len(BLOCKS), 2)
    ]

    def pair_terms(at):
        block, cell, c, same = met[at]

        def some(step, carry):
            first = pl.multiple_of(step * ROWS, ROWS)
            local = pl.ds(first, ROWS)
            found = jnp.dot(near[block, cell, local, :], reach[c], preferred_element_type=jnp.float32)
            s, scaled, left = (found[:, at * slots : (at + 1) * slots] for at in range(3))
            inv = lax.rsqrt(s)
            minus_x = scaled * (s * inv)
            e = jnp.exp(minus_x)
            t = jnp.maximum(left, 0.0) * inv
            w = t * t * inv
            if same:
                mine = stat[7:8, c * slots : (c + 1) * slots]
                theirs = jnp.concatenate([group[cell, local, :]] * tiles, axis=1)
                w = jnp.where(mine != theirs, w, 0.0)
            rest = 1.0 - e
            for which, term in enumerate((w * (inv * inv) * (rest + minus_x * e), w * rest)):
                high = term.astype(jnp.bfloat16)
                low = (term - high.astype(jnp.float32)).astype(jnp.bfloat16)
                pair[at, pl.ds(pl.multiple_of(2 * which * slots + first, ROWS), ROWS), :] = high
                pair[at, pl.ds(pl.multiple_of((2 * which + 1) * slots + first, ROWS), ROWS), :] = low
            return carry

        lax.fori_loop(0, slots // ROWS, some, 0, unroll=True)

    def pulled(at, sums):
        block, cell, c, _ = met[at]
        part = jnp.dot(pull[block, cell], pair[at], preferred_element_type=jnp.float32)
        sums[c] = part if sums[c] is None else sums[c] + part

    def field_rows(sums):
        found = []
        kind = jnp.bitwise_and(wide, 3)
        for c in range(cells):
            ax, ay, az = (place[0, c, m : m + 1, :] for m in range(3))
            total_sum = sum(sums[c][at * TERMS : (at + 1) * TERMS] for at in range(SPLITS))
            turn = jnp.where(kind == 0, 1.0, jnp.where(kind == 1, -ax, jnp.where(kind == 2, -ay, -az)))
            folded = [total_sum[at : at + SUBLANES] * turn for at in (0, SUBLANES)]
            base, hx, hy, hz = (
                jnp.sum(jnp.where((wide < 4) == side, part, 0.0), axis=0, keepdims=True)
                for part in folded
                for side in (True, False)
            )
            for m, (h, a) in enumerate(((hx, ax), (hy, ay), (hz, az))):
                row = h - a * base
                for tile in range(tiles):
                    found.append(row[:, tile * LANES : (tile + 1) * LANES])
        return found

    def jacobi_rows(fields):
        found = []
        for at, field in enumerate(fields):
            cell, m, tile, first = whereabouts(at)
            whole = permanent[m, cell : cell + 1, tile * LANES : (tile + 1) * LANES] + field * (1.0 / CUTOFF_SQ**2)
            found.append(scale[0:1, first : first + LANES] * whole)
        return found

    def whereabouts(at):
        cell, rest = divmod(at, 3 * tiles)
        m, tile = divmod(rest, tiles)
        return cell, m, tile, cell * slots + tile * LANES

    def as_row(column):
        return jnp.sum(jnp.where(sub == lane, column, 0.0), axis=0, keepdims=True)

    def mirrored(gram, row, k):
        column = jnp.sum(jnp.where(sub == lane, row, 0.0), axis=1, keepdims=True)
        return jnp.where(lane == k, column, jnp.where(sub == k, row, gram))

    def factor(gram, slot):
        rest = jnp.where(jnp.logical_or(sub == slot, lane == slot), jnp.where(sub == lane, 1.0, 0.0), gram)
        held = jnp.where(lane < SUBLANES, jnp.where(sub == lane, 1.0, 0.0), pltpu.roll(rest, SUBLANES, 1))
        for k in range(SUBLANES):
            column = jnp.broadcast_to(held[:, SUBLANES + k : SUBLANES + k + 1], held.shape)
            pivot_row = held[k : k + 1, :] / column[k : k + 1, :]
            held = jnp.where(sub == k, pivot_row, held - column * pivot_row)
        inverse = jnp.where(jnp.logical_and(lane < SUBLANES, lane != slot), held, 0.0)
        ones = jnp.sum(inverse, axis=1, keepdims=True)
        return slot, inverse, ones, as_row(ones), jnp.sum(ones, axis=0, keepdims=True)

    def solve(factored, row):
        slot, inverse, ones, ones_row, ones_sum = factored
        last = jnp.sum(jnp.where(lane[:1] == slot, row, 0.0), axis=1, keepdims=True)
        turned_row = jnp.sum(inverse * row, axis=1, keepdims=True)
        column = jnp.sum(jnp.where(jnp.logical_and(sub == lane, lane != slot), row, 0.0), axis=1, keepdims=True)
        cross = jnp.sum(ones_row * row, axis=1, keepdims=True)
        newest_y = (1.0 - cross) / (last - jnp.sum(column * turned_row, axis=0, keepdims=True))
        y = jnp.where(sub == slot, newest_y, ones - turned_row * newest_y)
        return y / (ones_sum + newest_y - cross * newest_y)

    def mixed(hist, weights, chunk):
        return jnp.sum(weights * hist, axis=0, keepdims=True)

    newest = SUBLANES - 1
    pl.semaphore_wait(barrier, total - 1)
    stat_copies = halo_copies(stat, stat_halo, stat_sem)
    for copy in stat_copies:
        copy.start()

    sums = [None] * cells
    waiting = []
    for at, blocks in enumerate(STAGES):
        for block in blocks:
            if block:
                arrived(stat_halo, stat_sem, block)
        for block in blocks:
            block_stat = stat_halo.at[landing(block)] if block else stat
            if block:
                prepare(block, block_stat)
            for cell in range(cells):
                span = slice(cell * slots, (cell + 1) * slots)
                lines(block, cell, [block_stat[4 + m : 5 + m, span] for m in range(3)])
        for one in range(len(met)):
            if met[one][0] in blocks:
                pair_terms(one)
                waiting.append(one)
                if len(waiting) > 1:
                    pulled(waiting.pop(0), sums)
        if at == HIST_AT:
            start_past()
            for copy in hist_copies:
                copy.start()
    for one in waiting:
        pulled(one, sums)

    jacobi = jacobi_rows(field_rows(sums))
    for row, chunk in zip(jacobi, chunks):
        jac_own[0:1, chunk] = row
    jac_copies = halo_copies(jac_own, jac_halo, jac_sem)
    residual = []
    for at, chunk in enumerate(chunks):
        cell, rest = divmod(at, 3 * tiles)
        m, tile = divmod(rest, tiles)
        first = cell * slots + tile * LANES
        residual.append(jacobi[at] - stat[4 + m : 5 + m, first : first + LANES])
    res_rows = [jnp.where(sub == newest, r, rows) for r, rows in zip(residual, hist_rows)]
    row = as_row(inner(res_rows, residual))
    start, finish, first_sent = share(row, row_send.at[0], row_recv.at[0], row_sem.at[0])
    for copy in jac_copies:
        copy.start()
    start()
    begun = set()
    sums = [None] * cells

    def hand_on(block):
        arrived(hist_halo, hist_sem, block)
        handed[block // 2 - 1].start()

    def met_in(block):
        return [at for at in range(len(met)) if met[at][0] == block]

    def stored_stage(block):
        if block % 2:
            arrived(hist_halo, hist_sem, block)
        hist = hist_halo.at[landing(block)] if block else out_hist
        for cell in range(cells):
            stored_lines(block, cell, hist)
        for at in met_in(block):
            stored_pulled(at, begun)

    def jacobi_stage(block):
        source = jac_halo.at[landing(block)] if block else jac_own
        for cell in range(cells):
            starts = [(cell * 3 + m) * slots for m in range(3)]
            lines(block, cell, [source[0:1, at : at + slots] for at in starts])
        for at in met_in(block):
            pulled(at, sums)

    hand_on(2)
    stored_stage(0)
    jacobi_stage(0)
    stored_stage(1)
    hand_on(4)
    past_gram = finish_past()
    factored = factor(past_gram, newest)
    stored_stage(2)
    arrived(jac_halo, jac_sem, 1)
    jacobi_stage(1)
    stored_stage(3)
    stored_stage(4)
    arrived(jac_halo, jac_sem, 2)
    arrived(jac_halo, jac_sem, 3)
    jacobi_stage(2)
    jacobi_stage(3)
    stored_stage(5)
    stored_fields()
    arrived(jac_halo, jac_sem, 4)
    arrived(jac_halo, jac_sem, 5)
    row = finish()
    jacobi_stage(4)
    jacobi_stage(5)
    weights = solve(factored, row)
    gram = mirrored(past_gram, row, newest)
    fields = [
        mixed(stored_field[:, chunk], weights, chunk) + weights[newest : newest + 1] * field
        for chunk, field in zip(chunks, field_rows(sums))
    ]
    current = [
        mixed(out_hist[:, chunk], weights, chunk) + weights[newest : newest + 1] * row
        for chunk, row in zip(chunks, jacobi)
    ]
    jacobi_next = jacobi_rows(fields)
    residual = [a - b for a, b in zip(jacobi_next, current)]
    res_rows = [jnp.where(sub == 0, r, rows) for r, rows in zip(residual, res_rows)]
    row = as_row(inner(res_rows, residual))
    start, finish, second_sent = share(row, row_send.at[1], row_recv.at[1], row_sem.at[1])
    start()
    factored = factor(gram, 0)
    weights = solve(factored, finish())
    kept = jnp.where(sub == 0, 0.0, weights)
    for at, chunk in enumerate(chunks):
        cell, rest = divmod(at, 3 * tiles)
        m, tile = divmod(rest, tiles)
        next_ref[0, m, cell : cell + 1, tile * LANES : (tile + 1) * LANES] = (
            mixed(out_hist[:, chunk], kept, chunk)
            + weights[newest : newest + 1] * jac_own[0:1, chunk]
            + weights[0:1] * jacobi_next[at]
        )
    column = jnp.concatenate([weights[1:], weights[0:1]], axis=0)
    weight_ref[...] = as_row(column)[0, :SUBLANES]

    for copy in stat_copies + hist_copies + handed + jac_copies:
        copy.wait_send()
    past_sent()
    first_sent()
    second_sent()


def wired(arg_count, nx, ny, cells, slots, tile_width, counts_arg, *refs):
    args, rest = refs[:arg_count], refs[arg_count:]
    outs, rest = rest[:2], rest[2:]
    held, rest = rest[:arg_count], rest[arg_count:]
    counts, *rest = rest
    args, inside = (*args, counts_arg), (*held, counts)
    kernel(nx, ny, cells, slots, tile_width, args, outs, inside, *rest)


def hand_over(current, weights, next_ref, weight_ref):
    next_ref[...] = current[...]
    weight_ref[...] = weights[...]


def body(nx, ny, positions, polarizability, tile_counts, molecules, perm_field, dipoles, past_out, past_res):
    cells, tile_count = tile_counts.shape[1:]
    slots = positions.shape[-1]
    tile_width = slots // tile_count
    tiles = slots // LANES
    past = past_out.shape[2]
    assert ny == 2 and nx > 2 and cells > 1 and past + 1 == SUBLANES and slots % LANES == 0
    width = cells * 3 * slots

    halo = len(BLOCKS) - 1
    met = 3 * (3 * cells)
    vmem = pl.BlockSpec(memory_space=pltpu.VMEM)
    hbm = pl.BlockSpec(memory_space=pltpu.HBM)
    raw = (
        jnp.swapaxes(positions, 1, 2),
        polarizability,
        molecules,
        jnp.swapaxes(perm_field, 1, 2),
        jnp.swapaxes(dipoles, 1, 2),
        jnp.transpose(past_out, (0, 2, 3, 1, 4)),
        jnp.transpose(past_res, (0, 2, 3, 1, 4)),
    )
    tile_counts, *raw = (
        pltpu.with_memory_space_constraint(arg, pltpu.HBM) for arg in (tile_counts, *raw)
    )
    pairs_kept = met * slots * slots
    current, weights = pl.pallas_call(
        functools.partial(wired, len(raw), nx, ny, cells, slots, tile_width),
        out_shape=(
            jax.ShapeDtypeStruct((1, 3, cells, slots), jnp.float32),
            jax.ShapeDtypeStruct((SUBLANES,), jnp.float32),
        ),
        in_specs=[hbm] * (1 + len(raw)),
        out_specs=(vmem, vmem),
        scratch_shapes=[pltpu.VMEM(arg.shape[1:], arg.dtype) for arg in raw]
        + [
            pltpu.SMEM(tile_counts.shape[1:], tile_counts.dtype),
            pltpu.VMEM((SUBLANES, cells * slots), jnp.float32),
            pltpu.VMEM((SUBLANES, width), jnp.float32),
            pltpu.VMEM((SUBLANES, width), jnp.float32),
            pltpu.VMEM((1, cells * slots), jnp.float32),
            pltpu.VMEM((halo, SUBLANES, cells * slots), jnp.float32),
            pltpu.VMEM((halo, SUBLANES, width), jnp.float32),
            pltpu.VMEM((halo, 1, width), jnp.float32),
            pltpu.VMEM((halo + 1, cells, SUBLANES, slots), jnp.float32),
            pltpu.VMEM((halo + 1, cells, slots, 2 * DEPTH), jnp.bfloat16),
            pltpu.VMEM((cells, slots, LANES), jnp.float32),
            pltpu.VMEM((halo + 1, cells, SPLITS * TERMS, 4 * slots), jnp.bfloat16),
            pltpu.VMEM((met, 4 * slots, slots), jnp.bfloat16),
            pltpu.VMEM((halo + 1, cells, 2 * TERMS * SUBLANES, 2 * slots), jnp.bfloat16),
            pltpu.VMEM((halo + 1, cells, 2 * 3 * SUBLANES, 2 * slots), jnp.bfloat16),
            pltpu.VMEM((cells, 2 * TERMS * SUBLANES, slots), jnp.float32),
            pltpu.VMEM((cells, 2 * 3 * SUBLANES, slots), jnp.float32),
            pltpu.VMEM((SUBLANES, width), jnp.float32),
            pltpu.VMEM((1, width), jnp.float32),
            pltpu.VMEM((SUBLANES, LANES), jnp.float32),
            pltpu.VMEM((nx * ny - 1, SUBLANES, LANES), jnp.float32),
            pltpu.VMEM((2, 1, LANES), jnp.float32),
            pltpu.VMEM((2, nx * ny - 1, 1, LANES), jnp.float32),
            pltpu.SemaphoreType.DMA((len(raw) + 1,)),
            pltpu.SemaphoreType.DMA((2, halo)),
            pltpu.SemaphoreType.DMA((2, halo)),
            pltpu.SemaphoreType.DMA((2, halo)),
            pltpu.SemaphoreType.DMA((2,)),
            pltpu.SemaphoreType.DMA((2, 2)),
        ],
        compiler_params=pltpu.CompilerParams(
            collective_id=0, has_side_effects=True, vmem_limit_bytes=32 * 1024 * 1024
        ),
        cost_estimate=pl.CostEstimate(
            flops=70 * pairs_kept, bytes_accessed=16 * width * SUBLANES, transcendentals=2 * pairs_kept
        ),
    )(tile_counts, *raw)
    current, weights = pl.pallas_call(
        hand_over,
        out_shape=(
            jax.ShapeDtypeStruct(current.shape, current.dtype),
            jax.ShapeDtypeStruct(weights.shape, weights.dtype),
        ),
        in_specs=[vmem] * 2,
        out_specs=(vmem, vmem),
        compiler_params=pltpu.CompilerParams(vmem_limit_bytes=1024 * 1024),

    )(current, weights)
    return (jnp.swapaxes(current, 1, 2), weights)


def solution(mesh):
    cell_axes = P(("box", "gx"), "gy")
    return jax.shard_map(
        functools.partial(body, mesh.shape["gx"], mesh.shape["gy"]),
        mesh=mesh,
        in_specs=(cell_axes,) * 8,
        out_specs=(cell_axes, P("box")),
        check_vma=False,
    )
```

```python
import functools

import jax
import jax.numpy as jnp
from jax import lax
from jax.experimental import pallas as pl
from jax.experimental.pallas import tpu as pltpu
from jax.sharding import PartitionSpec as P

CELL_SIDE = 9.0
CUTOFF_SQ = 81.0
SOFTENING = 0.25
THOLE_DAMP = 0.39
LANES = 128
SUBLANES = 8
ROWS = 32
DEPTH = 48
SPLITS = 3
TERMS = 16
MESH = pl.DeviceIdType.MESH

HIST_AT = 1
STAGES = ((0,), (1,), (2, 3), (4, 5))
BLOCKS = ((0, 0), (0, 1), (1, 0), (1, 1), (-1, 0), (-1, 1))


def block_row(cell, half, cells):
    if half == 0:
        return cell
    return -1 if cell == cells - 1 else cells


def kernel(
    nx,
    ny,
    cells,
    slots,
    tile_width,
    args,
    outs,
    held,
    stat,
    out_hist,
    res_hist,
    scale,
    stat_halo,
    hist_halo,
    jac_halo,
    place,
    near,
    group,
    pull,
    pair,
    stored_pull,
    stored_iso,
    stored_acc,
    stored_iso_acc,
    stored_field,
    jac_own,
    past_send,
    past_recv,
    row_send,
    row_recv,
    in_sem,
    stat_sem,
    hist_sem,
    jac_sem,
    past_sem,
    row_sem,
):
    next_ref, weight_ref = outs
    positions, polarity, molecules, permanent, dipoles, past_out, past_res, counts = held
    tiles = slots // LANES
    width = cells * 3 * slots
    total = nx * ny
    my_x = lax.axis_index("gx")
    my_y = lax.axis_index("gy")

    barrier = pltpu.get_barrier_semaphore()
    fetches = [
        pltpu.make_async_copy(arg.at[0], into, in_sem.at[at])
        for at, (arg, into) in enumerate(zip(args, held))
    ]
    for fetch in fetches:
        fetch.start()

    few = total <= 2 * SUBLANES

    def to_all(act):
        def both(step, carry):
            for ahead in (step, nx - step):
                column = my_x + ahead
                column = jnp.where(column >= nx, column - nx, column)
                for across in range(ny):
                    act(ahead * ny + across - 1, {"gx": column, "gy": jnp.where(my_y + across >= ny, 0, my_y + across)})
            return carry

        lax.fori_loop(1, nx // 2, both, 0, unroll=few)
        column = jnp.where(my_x >= nx // 2, my_x - nx // 2, my_x + nx // 2)
        for across in range(ny):
            act(nx // 2 * ny + across - 1, {"gx": column, "gy": jnp.where(my_y + across >= ny, 0, my_y + across)})
        act(0, {"gx": my_x, "gy": 1 - my_y})

    def greet(slot, target):
        pl.semaphore_signal(barrier, inc=1, device_id=target, device_id_type=MESH)

    to_all(greet)

    def halo_copies(source, landing, sems):
        copies = []
        for at, (x_offset, half) in enumerate(BLOCKS[1:]):
            target = {
                "gx": lax.rem(my_x - x_offset + nx, nx),
                "gy": lax.rem(my_y + half, ny),
            }
            copies.append(
                pltpu.make_async_remote_copy(
                    src_ref=source,
                    dst_ref=landing.at[at],
                    send_sem=sems.at[0, at],
                    recv_sem=sems.at[1, at],
                    device_id=target,
                    device_id_type=MESH,
                )
            )
        return copies

    index = lax.broadcasted_iota(jnp.int32, (1, slots), 1)
    for fetch in fetches:
        fetch.wait()
    occupied = []
    for cell in range(cells):
        live = jnp.zeros((1, slots), jnp.float32)
        for tile in range(slots // tile_width):
            first = tile * tile_width
            inside = jnp.logical_and(index >= first, index < first + counts[cell, tile])
            live = jnp.where(inside, 1.0, live)
        occupied.append(live)

    for cell in range(cells):
        span = slice(cell * slots, (cell + 1) * slots)
        polar = polarity[cell : cell + 1, :]
        for m in range(3):
            stat[m : m + 1, span] = positions[m, cell : cell + 1, :]
            stat[4 + m : 5 + m, span] = dipoles[m, cell : cell + 1, :] * occupied[cell]
        stat[3:4, span] = lax.rsqrt(polar)
        stat[7:8, span] = molecules[cell : cell + 1, :].astype(jnp.float32)
        scale[0:1, span] = polar * occupied[cell]

    for stored, hist in ((past_res, res_hist), (past_out, out_hist)):
        hist[SUBLANES - 1 :, :] = jnp.zeros((1, width), jnp.float32)
        for cell in range(cells):
            for m in range(3):
                first = (cell * 3 + m) * slots
                for k in range(SUBLANES - 1):
                    row = stored[k, m, cell : cell + 1, :] * occupied[cell]
                    hist[k : k + 1, first : first + slots] = row

    wide = lax.broadcasted_iota(jnp.int32, (SUBLANES, slots), 0)
    centre = CELL_SIDE * 0.5

    def split(values):
        high = values.astype(jnp.bfloat16)
        rest = values - high.astype(jnp.float32)
        mid = rest.astype(jnp.bfloat16)
        low = (rest - mid.astype(jnp.float32)).astype(jnp.bfloat16)
        return high, mid, low

    def located(rows, x_shift, y_shift):
        shift = jnp.where(wide == 0, x_shift - centre, jnp.where(wide == 1, y_shift - cells * centre, -tiles * centre))
        moved = jnp.where(wide < 3, rows + shift, 0.0)
        return moved, jnp.sum(moved * moved, axis=0, keepdims=True)

    def in_row(at, value, rows):
        return jnp.where(wide == at, value, rows)

    turned = my_x == nx - 1
    swap = jnp.where(turned, 1, 0)

    def landing(block):
        return block - 1 if block < 2 else 2 * jnp.where(block < 4, swap, 1 - swap) + block % 2 + 1

    def arrived(landed, sems, block):
        into = landed.at[landing(block)]
        pltpu.make_async_copy(into, into, sems.at[1, landing(block)]).wait()

    def prepare(block, block_stat):
        x_offset, half = BLOCKS[block]
        x_offset = jnp.where(turned, -x_offset, x_offset).astype(jnp.float32)
        for cell in range(cells):
            rows = block_stat[:, cell * slots : (cell + 1) * slots]
            moved, norm = located(rows, CELL_SIDE * x_offset, CELL_SIDE * block_row(cell, half, cells))
            place[block, cell] = moved
            sides = in_row(3, 1.0, in_row(4, norm, moved))
            stack = []
            for values in (sides, sides * rows[3:4, :]):
                high, mid, low = (part.astype(jnp.float32) for part in split(values))
                stack += [high, mid, high, low, high, mid]
            if block == 0:
                stack.append(rows)
            columns = jnp.transpose(jnp.concatenate(stack, axis=0))
            near[block, cell] = columns[:, : 2 * DEPTH].astype(jnp.bfloat16)
            if block == 0:
                group[cell] = jnp.broadcast_to(columns[:, 2 * DEPTH + 7 : 2 * DEPTH + 8], (slots, LANES))

    def lines(block, cell, vector):
        bx, by, bz = (place[block, cell, m : m + 1, :] for m in range(3))
        vx, vy, vz = (3.0 * v for v in vector)
        dot = bx * vx + by * vy + bz * vz
        kind = jnp.bitwise_and(wide, 3)
        right = jnp.where(kind == 0, dot, jnp.where(kind == 1, vx, jnp.where(kind == 2, vy, vz)))
        upper = wide < 4
        outer = jnp.concatenate(
            [jnp.where(upper, 1.0, bx) * right, jnp.where(upper, by, bz) * right], axis=0
        )
        ux, uy, uz = vector
        plain = jnp.concatenate(
            [in_row(4, -ux, 0.0), in_row(0, -uy, in_row(4, -uz, 0.0))], axis=0
        )
        for at, part in enumerate(zip(split(outer), split(plain))):
            for which, term in enumerate(part):
                for copy in range(2):
                    first = (2 * which + copy) * slots
                    pull[block, cell, at * TERMS : (at + 1) * TERMS, first : first + slots] = term

    def stored_lines(block, cell, hist):
        bx, by, bz = (place[block, cell, m : m + 1, :] for m in range(3))
        plain = [hist[:, (cell * 3 + m) * slots : (cell * 3 + m + 1) * slots] for m in range(3)]
        vx, vy, vz = (3.0 * v for v in plain)
        right = (bx * vx + by * vy + bz * vz, vx, vy, vz)
        outer = [r if left is None else left * r for left in (None, bx, by, bz) for r in right]
        for into, rows in ((stored_pull, outer), (stored_iso, [-v for v in plain])):
            values = jnp.concatenate(rows, axis=0)
            high, mid, _ = split(values)
            both = jnp.concatenate([high.astype(jnp.float32), mid.astype(jnp.float32)], axis=0)
            both = both.astype(jnp.bfloat16)
            for copy in range(2):
                into[block, cell, :, copy * slots : (copy + 1) * slots] = both

    def stored_pulled(at, begun):
        block, cell, c, _ = met[at]
        for left, acc, first in ((stored_pull, stored_acc, 0), (stored_iso, stored_iso_acc, 2 * slots)):
            part = jnp.dot(
                left[block, cell], pair[at, first : first + 2 * slots, :], preferred_element_type=jnp.float32
            )
            acc[c] = acc[c] + part if c in begun else part
        begun.add(c)

    def stored_fields():
        for c in range(cells):
            ax, ay, az = (place[0, c, m : m + 1, :] for m in range(3))

            def term(at):
                first, second = at * SUBLANES, (TERMS + at) * SUBLANES
                return stored_acc[c, first : first + SUBLANES, :] + stored_acc[c, second : second + SUBLANES, :]

            base, hx, hy, hz = (
                term(4 * i) - ax * term(4 * i + 1) - ay * term(4 * i + 2) - az * term(4 * i + 3) for i in range(4)
            )
            for m, (h, a) in enumerate(((hx, ax), (hy, ay), (hz, az))):
                first, second = m * SUBLANES, (3 + m) * SUBLANES
                iso = stored_iso_acc[c, first : first + SUBLANES, :] + stored_iso_acc[c, second : second + SUBLANES, :]
                stored_field[:, (c * 3 + m) * slots : (c * 3 + m + 1) * slots] = h - a * base + iso

    def toward(target):
        rows = stat[:, target * slots : (target + 1) * slots]
        moved, norm = located(rows, 0.0, CELL_SIDE * target)
        norm = norm + SOFTENING
        sides = in_row(3, norm, in_row(4, 1.0, -2.0 * moved))
        blank = jnp.zeros((DEPTH, slots), jnp.bfloat16)
        columns = []
        for values, first in (
            (sides, True),
            (sides * (-THOLE_DAMP * rows[3:4, :]), False),
            (in_row(3, CUTOFF_SQ - norm, -sides), True),
        ):
            high, mid, low = (part.astype(jnp.float32) for part in split(values))
            part = jnp.concatenate([high, high, mid, high, low, mid], axis=0).astype(jnp.bfloat16)
            columns.append(jnp.concatenate([part, blank] if first else [blank, part], axis=0))
        return jnp.concatenate(columns, axis=1)

    prepare(0, stat)
    reach = [toward(c) for c in range(cells)]

    sub = lax.broadcasted_iota(jnp.int32, (SUBLANES, LANES), 0)
    lane = lax.broadcasted_iota(jnp.int32, (SUBLANES, LANES), 1)
    chunks = [slice(at * LANES, (at + 1) * LANES) for at in range(width // LANES)]

    def inner(rows, vector):
        parts = [r * v for r, v in zip(rows, vector)]
        while len(parts) > 1:
            parts = [sum(parts[at : at + 2]) for at in range(0, len(parts), 2)]
        return jnp.sum(parts[0], axis=1, keepdims=True)

    hist_rows = [res_hist[:, chunk] for chunk in chunks]
    past_gram = jnp.zeros((SUBLANES, LANES), jnp.float32)
    for k in range(SUBLANES - 1):
        column = inner(hist_rows, [rows[k : k + 1] for rows in hist_rows])
        past_gram = past_gram + jnp.where(lane == k, column, 0.0)

    met = [
        (block, cell, c, block == 0 and cell == c)
        for block in range(len(BLOCKS))
        for c in range(cells)
        for cell in range(cells)
        if (BLOCKS[block][1] == 0 or cell in (0, cells - 1))
        and abs(block_row(cell, BLOCKS[block][1], cells) - c) <= 1
    ]

    def share(mine, sent, landed, sems):
        sent[...] = mine

        def send(slot, target):
            pltpu.make_async_remote_copy(
                src_ref=sent,
                dst_ref=landed.at[slot],
                send_sem=sems.at[0],
                recv_sem=sems.at[1],
                device_id=target,
                device_id_type=MESH,
            ).start()

        def start():
            to_all(send)

        def finish():
            pltpu.make_async_copy(landed, landed, sems.at[1]).wait()
            return mine + jnp.sum(landed[...], axis=0)

        def sent_all():
            pltpu.make_async_copy(landed, landed, sems.at[0]).wait()

        return start, finish, sent_all

    start_past, finish_past, past_sent = share(past_gram, past_send, past_recv, past_sem)
    hist_copies = [
        copy for at, copy in enumerate(halo_copies(out_hist, hist_halo, hist_sem)) if at == 0 or at % 2
    ]
    handed = [
        pltpu.make_async_remote_copy(
            src_ref=hist_halo.at[landing(block)],
            dst_ref=hist_halo.at[landing(block) + 1],
            send_sem=hist_sem.at[0, landing(block) + 1],
            recv_sem=hist_sem.at[1, landing(block) + 1],
            device_id={"gx": my_x, "gy": 1 - my_y},
            device_id_type=MESH,
        )
        for block in range(2, len(BLOCKS), 2)
    ]

    def pair_terms(at):
        block, cell, c, same = met[at]

        def some(step, carry):
            first = pl.multiple_of(step * ROWS, ROWS)
            local = pl.ds(first, ROWS)
            found = jnp.dot(near[block, cell, local, :], reach[c], preferred_element_type=jnp.float32)
            s, scaled, left = (found[:, at * slots : (at + 1) * slots] for at in range(3))
            inv = lax.rsqrt(s)
            minus_x = scaled * (s * inv)
            e = jnp.exp(minus_x)
            t = jnp.maximum(left, 0.0) * inv
            w = t * t * inv
            if same:
                mine = stat[7:8, c * slots : (c + 1) * slots]
                theirs = jnp.concatenate([group[cell, local, :]] * tiles, axis=1)
                w = jnp.where(mine != theirs, w, 0.0)
            rest = 1.0 - e
            for which, term in enumerate((w * (inv * inv) * (rest + minus_x * e), w * rest)):
                high = term.astype(jnp.bfloat16)
                low = (term - high.astype(jnp.float32)).astype(jnp.bfloat16)
                pair[at, pl.ds(pl.multiple_of(2 * which * slots + first, ROWS), ROWS), :] = high
                pair[at, pl.ds(pl.multiple_of((2 * which + 1) * slots + first, ROWS), ROWS), :] = low
            return carry

        lax.fori_loop(0, slots // ROWS, some, 0, unroll=True)

    def pulled(at, sums):
        block, cell, c, _ = met[at]
        part = jnp.dot(pull[block, cell], pair[at], preferred_element_type=jnp.float32)
        sums[c] = part if sums[c] is None else sums[c] + part

    def field_rows(sums):
        found = []
        kind = jnp.bitwise_and(wide, 3)
        for c in range(cells):
            ax, ay, az = (place[0, c, m : m + 1, :] for m in range(3))
            total_sum = sum(sums[c][at * TERMS : (at + 1) * TERMS] for at in range(SPLITS))
            turn = jnp.where(kind == 0, 1.0, jnp.where(kind == 1, -ax, jnp.where(kind == 2, -ay, -az)))
            folded = [total_sum[at : at + SUBLANES] * turn for at in (0, SUBLANES)]
            base, hx, hy, hz = (
                jnp.sum(jnp.where((wide < 4) == side, part, 0.0), axis=0, keepdims=True)
                for part in folded
                for side in (True, False)
            )
            for m, (h, a) in enumerate(((hx, ax), (hy, ay), (hz, az))):
                row = h - a * base
                for tile in range(tiles):
                    found.append(row[:, tile * LANES : (tile + 1) * LANES])
        return found

    def jacobi_rows(fields):
        found = []
        for at, field in enumerate(fields):
            cell, m, tile, first = whereabouts(at)
            whole = permanent[m, cell : cell + 1, tile * LANES : (tile + 1) * LANES] + field * (1.0 / CUTOFF_SQ**2)
            found.append(scale[0:1, first : first + LANES] * whole)
        return found

    def whereabouts(at):
        cell, rest = divmod(at, 3 * tiles)
        m, tile = divmod(rest, tiles)
        return cell, m, tile, cell * slots + tile * LANES

    def as_row(column):
        return jnp.sum(jnp.where(sub == lane, column, 0.0), axis=0, keepdims=True)

    def mirrored(gram, row, k):
        column = jnp.sum(jnp.where(sub == lane, row, 0.0), axis=1, keepdims=True)
        return jnp.where(lane == k, column, jnp.where(sub == k, row, gram))

    def factor(gram, slot):
        rest = jnp.where(jnp.logical_or(sub == slot, lane == slot), jnp.where(sub == lane, 1.0, 0.0), gram)
        held = jnp.where(lane < SUBLANES, jnp.where(sub == lane, 1.0, 0.0), pltpu.roll(rest, SUBLANES, 1))
        for k in range(SUBLANES):
            column = jnp.broadcast_to(held[:, SUBLANES + k : SUBLANES + k + 1], held.shape)
            pivot_row = held[k : k + 1, :] / column[k : k + 1, :]
            held = jnp.where(sub == k, pivot_row, held - column * pivot_row)
        inverse = jnp.where(jnp.logical_and(lane < SUBLANES, lane != slot), held, 0.0)
        ones = jnp.sum(inverse, axis=1, keepdims=True)
        return slot, inverse, ones, as_row(ones), jnp.sum(ones, axis=0, keepdims=True)

    def solve(factored, row):
        slot, inverse, ones, ones_row, ones_sum = factored
        last = jnp.sum(jnp.where(lane[:1] == slot, row, 0.0), axis=1, keepdims=True)
        turned_row = jnp.sum(inverse * row, axis=1, keepdims=True)
        column = jnp.sum(jnp.where(jnp.logical_and(sub == lane, lane != slot), row, 0.0), axis=1, keepdims=True)
        cross = jnp.sum(ones_row * row, axis=1, keepdims=True)
        newest_y = (1.0 - cross) / (last - jnp.sum(column * turned_row, axis=0, keepdims=True))
        y = jnp.where(sub == slot, newest_y, ones - turned_row * newest_y)
        return y / (ones_sum + newest_y - cross * newest_y)

    def mixed(hist, weights, chunk):
        return jnp.sum(weights * hist, axis=0, keepdims=True)

    newest = SUBLANES - 1
    sums = [None] * cells
    waiting = []
    for at, blocks in enumerate(STAGES):
        for block in blocks:
            if block:
                arrived(stat_halo, stat_sem, block)
        for block in blocks:
            block_stat = stat_halo.at[landing(block)] if block else stat
            if block:
                prepare(block, block_stat)
            for cell in range(cells):
                span = slice(cell * slots, (cell + 1) * slots)
                lines(block, cell, [block_stat[4 + m : 5 + m, span] for m in range(3)])
        for one in range(len(met)):
            if met[one][0] in blocks:
                pair_terms(one)
                waiting.append(one)
                if len(waiting) > 1:
                    pulled(waiting.pop(0), sums)
        if at == 0:
            pl.semaphore_wait(barrier, total - 1)
            stat_copies = halo_copies(stat, stat_halo, stat_sem)
            for copy in stat_copies:
                copy.start()

        if at == HIST_AT:
            start_past()
            for copy in hist_copies:
                copy.start()
    for one in waiting:
        pulled(one, sums)

    jacobi = jacobi_rows(field_rows(sums))
    for row, chunk in zip(jacobi, chunks):
        jac_own[0:1, chunk] = row
    jac_copies = halo_copies(jac_own, jac_halo, jac_sem)
    residual = []
    for at, chunk in enumerate(chunks):
        cell, rest = divmod(at, 3 * tiles)
        m, tile = divmod(rest, tiles)
        first = cell * slots + tile * LANES
        residual.append(jacobi[at] - stat[4 + m : 5 + m, first : first + LANES])
    res_rows = [jnp.where(sub == newest, r, rows) for r, rows in zip(residual, hist_rows)]
    row = as_row(inner(res_rows, residual))
    start, finish, first_sent = share(row, row_send.at[0], row_recv.at[0], row_sem.at[0])
    for copy in jac_copies:
        copy.start()
    start()
    begun = set()
    sums = [None] * cells

    def hand_on(block):
        arrived(hist_halo, hist_sem, block)
        handed[block // 2 - 1].start()

    def met_in(block):
        return [at for at in range(len(met)) if met[at][0] == block]

    def stored_stage(block):
        if block % 2:
            arrived(hist_halo, hist_sem, block)
        hist = hist_halo.at[landing(block)] if block else out_hist
        for cell in range(cells):
            stored_lines(block, cell, hist)
        for at in met_in(block):
            stored_pulled(at, begun)

    def jacobi_stage(block):
        source = jac_halo.at[landing(block)] if block else jac_own
        for cell in range(cells):
            starts = [(cell * 3 + m) * slots for m in range(3)]
            lines(block, cell, [source[0:1, at : at + slots] for at in starts])
        for at in met_in(block):
            pulled(at, sums)

    hand_on(2)
    stored_stage(0)
    jacobi_stage(0)
    stored_stage(1)
    hand_on(4)
    past_gram = finish_past()
    factored = factor(past_gram, newest)
    stored_stage(2)
    arrived(jac_halo, jac_sem, 1)
    jacobi_stage(1)
    stored_stage(3)
    stored_stage(4)
    arrived(jac_halo, jac_sem, 2)
    arrived(jac_halo, jac_sem, 3)
    jacobi_stage(2)
    jacobi_stage(3)
    stored_stage(5)
    stored_fields()
    arrived(jac_halo, jac_sem, 4)
    arrived(jac_halo, jac_sem, 5)
    row = finish()
    jacobi_stage(4)
    jacobi_stage(5)
    weights = solve(factored, row)
    gram = mirrored(past_gram, row, newest)
    fields = [
        mixed(stored_field[:, chunk], weights, chunk) + weights[newest : newest + 1] * field
        for chunk, field in zip(chunks, field_rows(sums))
    ]
    current = [
        mixed(out_hist[:, chunk], weights, chunk) + weights[newest : newest + 1] * row
        for chunk, row in zip(chunks, jacobi)
    ]
    jacobi_next = jacobi_rows(fields)
    residual = [a - b for a, b in zip(jacobi_next, current)]
    res_rows = [jnp.where(sub == 0, r, rows) for r, rows in zip(residual, res_rows)]
    row = as_row(inner(res_rows, residual))
    start, finish, second_sent = share(row, row_send.at[1], row_recv.at[1], row_sem.at[1])
    start()
    factored = factor(gram, 0)
    weights = solve(factored, finish())
    kept = jnp.where(sub == 0, 0.0, weights)
    for at, chunk in enumerate(chunks):
        cell, rest = divmod(at, 3 * tiles)
        m, tile = divmod(rest, tiles)
        next_ref[0, m, cell : cell + 1, tile * LANES : (tile + 1) * LANES] = (
            mixed(out_hist[:, chunk], kept, chunk)
            + weights[newest : newest + 1] * jac_own[0:1, chunk]
            + weights[0:1] * jacobi_next[at]
        )
    column = jnp.concatenate([weights[1:], weights[0:1]], axis=0)
    weight_ref[...] = as_row(column)[0, :SUBLANES]

    for copy in stat_copies + hist_copies + handed + jac_copies:
        copy.wait_send()
    past_sent()
    first_sent()
    second_sent()


def wired(arg_count, nx, ny, cells, slots, tile_width, counts_arg, *refs):
    args, rest = refs[:arg_count], refs[arg_count:]
    outs, rest = rest[:2], rest[2:]
    held, rest = rest[:arg_count], rest[arg_count:]
    counts, *rest = rest
    args, inside = (*args, counts_arg), (*held, counts)
    kernel(nx, ny, cells, slots, tile_width, args, outs, inside, *rest)


def hand_over(current, weights, next_ref, weight_ref):
    next_ref[...] = current[...]
    weight_ref[...] = weights[...]


def body(nx, ny, positions, polarizability, tile_counts, molecules, perm_field, dipoles, past_out, past_res):
    cells, tile_count = tile_counts.shape[1:]
    slots = positions.shape[-1]
    tile_width = slots // tile_count
    tiles = slots // LANES
    past = past_out.shape[2]
    assert ny == 2 and nx > 2 and cells > 1 and past + 1 == SUBLANES and slots % LANES == 0
    width = cells * 3 * slots

    halo = len(BLOCKS) - 1
    met = 3 * (3 * cells)
    vmem = pl.BlockSpec(memory_space=pltpu.VMEM)
    hbm = pl.BlockSpec(memory_space=pltpu.HBM)
    raw = (
        jnp.swapaxes(positions, 1, 2),
        polarizability,
        molecules,
        jnp.swapaxes(perm_field, 1, 2),
        jnp.swapaxes(dipoles, 1, 2),
        jnp.transpose(past_out, (0, 2, 3, 1, 4)),
        jnp.transpose(past_res, (0, 2, 3, 1, 4)),
    )
    tile_counts, *raw = (
        pltpu.with_memory_space_constraint(arg, pltpu.HBM) for arg in (tile_counts, *raw)
    )
    pairs_kept = met * slots * slots
    current, weights = pl.pallas_call(
        functools.partial(wired, len(raw), nx, ny, cells, slots, tile_width),
        out_shape=(
            jax.ShapeDtypeStruct((1, 3, cells, slots), jnp.float32),
            jax.ShapeDtypeStruct((SUBLANES,), jnp.float32),
        ),
        in_specs=[hbm] * (1 + len(raw)),
        out_specs=(vmem, vmem),
        scratch_shapes=[pltpu.VMEM(arg.shape[1:], arg.dtype) for arg in raw]
        + [
            pltpu.SMEM(tile_counts.shape[1:], tile_counts.dtype),
            pltpu.VMEM((SUBLANES, cells * slots), jnp.float32),
            pltpu.VMEM((SUBLANES, width), jnp.float32),
            pltpu.VMEM((SUBLANES, width), jnp.float32),
            pltpu.VMEM((1, cells * slots), jnp.float32),
            pltpu.VMEM((halo, SUBLANES, cells * slots), jnp.float32),
            pltpu.VMEM((halo, SUBLANES, width), jnp.float32),
            pltpu.VMEM((halo, 1, width), jnp.float32),
            pltpu.VMEM((halo + 1, cells, SUBLANES, slots), jnp.float32),
            pltpu.VMEM((halo + 1, cells, slots, 2 * DEPTH), jnp.bfloat16),
            pltpu.VMEM((cells, slots, LANES), jnp.float32),
            pltpu.VMEM((halo + 1, cells, SPLITS * TERMS, 4 * slots), jnp.bfloat16),
            pltpu.VMEM((met, 4 * slots, slots), jnp.bfloat16),
            pltpu.VMEM((halo + 1, cells, 2 * TERMS * SUBLANES, 2 * slots), jnp.bfloat16),
            pltpu.VMEM((halo + 1, cells, 2 * 3 * SUBLANES, 2 * slots), jnp.bfloat16),
            pltpu.VMEM((cells, 2 * TERMS * SUBLANES, slots), jnp.float32),
            pltpu.VMEM((cells, 2 * 3 * SUBLANES, slots), jnp.float32),
            pltpu.VMEM((SUBLANES, width), jnp.float32),
            pltpu.VMEM((1, width), jnp.float32),
            pltpu.VMEM((SUBLANES, LANES), jnp.float32),
            pltpu.VMEM((nx * ny - 1, SUBLANES, LANES), jnp.float32),
            pltpu.VMEM((2, 1, LANES), jnp.float32),
            pltpu.VMEM((2, nx * ny - 1, 1, LANES), jnp.float32),
            pltpu.SemaphoreType.DMA((len(raw) + 1,)),
            pltpu.SemaphoreType.DMA((2, halo)),
            pltpu.SemaphoreType.DMA((2, halo)),
            pltpu.SemaphoreType.DMA((2, halo)),
            pltpu.SemaphoreType.DMA((2,)),
            pltpu.SemaphoreType.DMA((2, 2)),
        ],
        compiler_params=pltpu.CompilerParams(
            collective_id=0, has_side_effects=True, vmem_limit_bytes=32 * 1024 * 1024
        ),
        cost_estimate=pl.CostEstimate(
            flops=70 * pairs_kept, bytes_accessed=16 * width * SUBLANES, transcendentals=2 * pairs_kept
        ),
    )(tile_counts, *raw)
    current, weights = pl.pallas_call(
        hand_over,
        out_shape=(
            jax.ShapeDtypeStruct(current.shape, current.dtype),
            jax.ShapeDtypeStruct(weights.shape, weights.dtype),
        ),
        in_specs=[vmem] * 2,
        out_specs=(vmem, vmem),
        compiler_params=pltpu.CompilerParams(vmem_limit_bytes=1024 * 1024),

    )(current, weights)
    return (jnp.swapaxes(current, 1, 2), weights)


def solution(mesh):
    cell_axes = P(("box", "gx"), "gy")
    return jax.shard_map(
        functools.partial(body, mesh.shape["gx"], mesh.shape["gy"]),
        mesh=mesh,
        in_specs=(cell_axes,) * 8,
        out_specs=(cell_axes, P("box")),
        check_vma=False,
    )
```
